32 devices in a mesh: pipe: 4 (over x, core), fsdp: 8 (over z, y).
Axes of the slice: x: 2, y: 2, z: 4, core: 2. Of those that a mesh axis runs over, the one named last changes fastest.
Arguments:
- saved: bfloat16 [4, 8, 3, 64, 4096], P('pipe', 'fsdp'), may hold values from -6 to 6
- cot_in: bfloat16 [4, 8, 64, 4096], P('pipe', 'fsdp'), may hold values from -6 to 6
- weights: bfloat16 [2, 4, 4096, 1024], P(None, 'pipe', 'fsdp'), may hold values from -0.09375 to 0.09375
- gains: bfloat16 [2, 4, 4096], P(None, 'pipe', 'fsdp'), may hold values from 0.099609375 to 1.8984375
- lengths: int32 [4, 8], P(None, 'fsdp'), may hold values from 1 to 64, 384 in all within a row
- segments: int32 [4, 8, 64], P(None, 'fsdp'), may hold values from 0 to 3, never falling along the last dimension, each value on 1 to 32 neighbouring positions
Outputs:
- cot_out: bfloat16 [4, 8, 64, 4096], P('pipe', 'fsdp')
- grad_kv: bfloat16 [2, 4, 4096, 1024], P(None, 'pipe', 'fsdp')
- grad_gain: bfloat16 [2, 4, 4096], P(None, 'pipe', 'fsdp')
The draws below stay inside these ranges and needn't reach their ends.
Inputs may be any that keep to these rules, and one draw needn't show every extreme that they name: The lengths of the 8 micro-batches of one j sum to 384 and the largest is 64. `segments`: document numbers never fall along the slots; a document spans at most 32 slots.
All inputs are finite; a program needn't handle non-finite values. No bound on the sum of `lengths` on one device may be relied on, other than what follows from the above.
Results may differ from the reference program's by a relative error of at most 0.02.
Values may be sent and summed in bfloat16 or wider, within the bound.
A program may use at most 128 MiB of HBM per device.

```python
import math
import jax
import jax.numpy as jnp
import numpy as np
from jax import lax

D = 4096
HEAD_SIZE = 128
KEY_VALUE_HEADS = 4
S = 64
TICKS = 3
KVW = 1024
N_PIPE = 4
N_FSDP = 8


def block_scale(rng, shape, cuts, least, largest):
    def one(axis_at, blocks):
        draws = jax.random.uniform(jax.random.fold_in(jax.random.fold_in(rng, 6), axis_at), (blocks,), jnp.float32, least / len(cuts), largest / len(cuts))
        return jnp.repeat(jnp.exp(draws), shape[axis_at] // blocks).reshape((-1,) + (1,) * (len(shape) - axis_at - 1))

    level = one(*cuts[0])
    for cut in cuts[1:]:
        level = level * one(*cut)
    return level


def length_profile(amount, total, reach, lean):
    loads = [(1 << 20) // math.isqrt(standing ** lean) + 1 for standing in range(2, amount + 1)]
    spare, holding = total - reach - (amount - 1), [1] * (amount - 1)
    while spare > 0:
        free = [i for i in range(amount - 1) if holding[i] < reach]
        mass, remaining = sum([loads[i] for i in free]), spare
        for i in free:
            more = min(reach - holding[i], max(1, remaining * loads[i] // mass), spare)
            holding[i] = holding[i] + more
            spare = spare - more
    return np.array([reach] + holding)


def ragged(stream_key, count, total, limit, skew):
    if count == 2:
        one = jax.random.randint(stream_key, (), max(1, total - limit), min(limit, total - 1) + 1)
        return jnp.stack([one, total - one])
    tallies = jnp.asarray(length_profile(count, total, limit, skew), jnp.int32)
    pairs = (count - 1) // 2
    donor, sink = tallies[1:1 + 2 * pairs:2], tallies[2:2 + 2 * pairs:2]
    room = jnp.minimum(donor - 1, limit - sink)
    moved = jax.random.randint(jax.random.fold_in(stream_key, 1), (pairs,), 0, 1 << 20) % (room + 1)
    tallies = tallies.at[1:1 + 2 * pairs:2].set(donor - moved).at[2:2 + 2 * pairs:2].set(sink + moved)
    return tallies[jax.random.permutation(jax.random.fold_in(stream_key, 2), count)]


def normal_values(stream_key, dims, deviation, limit, pieces=(), kind=jnp.bfloat16):
    result = deviation * jax.random.normal(stream_key, dims, jnp.float32)
    if pieces:
        result = result * block_scale(stream_key, dims, pieces, -0.22, 0.18)
    return jnp.clip(result, -limit, limit).astype(kind)


def setup_inputs(seed: int = 0) -> dict:
    key_list = jax.random.split(jax.random.key(seed), 7)
    return {
        "saved": normal_values(key_list[0], (N_PIPE, N_FSDP, TICKS, S, D), 1.0, 6.0, ((0, 4), (1, 8))),
        "cot_in": normal_values(key_list[1], (N_PIPE, N_FSDP, S, D), 1.0, 6.0, ((0, 4), (1, 8))),
        "weights": normal_values(key_list[2], (2, N_PIPE, D, KVW), D ** -0.5, 0.09375, ((1, 4), (2, 8))),
        "gains": jnp.clip(1.0 + 0.18 * jax.random.normal(key_list[3], (2, N_PIPE, D), jnp.float32), 0.099609375, 1.8984375).astype(jnp.bfloat16),
        "lengths": jax.vmap(lambda own: ragged(own, N_FSDP, 3 * N_FSDP * S // 4, S, 2))(jax.random.split(key_list[4], N_PIPE)).reshape((N_PIPE, N_FSDP)).astype(jnp.int32),
        "segments": jax.vmap(lambda own: jnp.searchsorted(jnp.cumsum(ragged(own, 4, S, S // 2, 1)), jnp.arange(S), side="right"))(jax.random.split(key_list[5], N_PIPE * N_FSDP)).reshape((N_PIPE, N_FSDP, S)).astype(jnp.int32),
    }


EPS = 1e-05

def normalize(resid, gain):
    factor = lax.rsqrt(lax.optimization_barrier(jnp.mean(resid * resid, axis=-1, keepdims=True)) + EPS)
    return resid * factor * gain

def attend(resid, normalized_input, key_value_pair, length, segment):
    item_count = resid.shape[0]
    model_width = resid.shape[1]
    query_groups = model_width // HEAD_SIZE // KEY_VALUE_HEADS
    query_rows = normalized_input.astype(jnp.bfloat16).reshape(item_count, KEY_VALUE_HEADS, query_groups, HEAD_SIZE)
    key_rows = key_value_pair[:, :KEY_VALUE_HEADS * HEAD_SIZE].astype(jnp.bfloat16).reshape(item_count, KEY_VALUE_HEADS, HEAD_SIZE)
    value_rows = key_value_pair[:, KEY_VALUE_HEADS * HEAD_SIZE:].astype(jnp.bfloat16).reshape(item_count, KEY_VALUE_HEADS, HEAD_SIZE)
    scores = jnp.einsum('pkgd,qkd->kgpq', query_rows, key_rows, preferred_element_type=jnp.float32) * HEAD_SIZE ** (-0.5)
    place = jnp.arange(item_count, dtype=jnp.int32)
    allowed = (segment[:, None] == segment[None, :]) & (place[None, :] <= place[:, None]) & (place[None, :] < length)
    allowed = allowed | (place[:, None] == place[None, :])
    scores = jnp.where(allowed, scores, -1e+30)
    peak = lax.optimization_barrier(jnp.max(scores, axis=-1, keepdims=True))
    expo = jnp.exp(scores - peak)
    probs = (expo / lax.optimization_barrier(jnp.sum(expo, axis=-1, keepdims=True))).astype(jnp.bfloat16)
    mixed = jnp.einsum('kgpq,qkd->pkgd', probs, value_rows, preferred_element_type=jnp.float32).reshape(item_count, model_width)
    valid = (place < length).astype(jnp.float32)
    return resid + mixed * valid[:, None]

def attend_back(resid, normalized_input, key_value_pair, cotangent, length, segment):

    def inner(first, second, third):
        return attend(first, second, third, length, segment)
    _, pull = jax.vjp(inner, resid, normalized_input, key_value_pair)
    direct, normed_cot, keyval_cot = pull(cotangent.astype(jnp.float32))
    return (direct, normed_cot, keyval_cot.astype(jnp.bfloat16))

def layer_back(saved_in, cotangent, gain, weight, length, segment):
    resid = saved_in.astype(jnp.float32)
    normalized_input, front_pull = jax.vjp(normalize, resid, gain.astype(jnp.float32))
    normed_b = normalized_input.astype(jnp.bfloat16)
    key_value_pair = jnp.dot(normed_b, weight, preferred_element_type=jnp.float32)
    direct, normed_cot, keyval_cot = attend_back(resid, normalized_input, key_value_pair, cotangent, length, segment)
    normed_total = normed_cot + jnp.dot(keyval_cot, weight.T, preferred_element_type=jnp.float32)
    resid_cot, gain_cot = front_pull(normed_total)
    fresh = (direct + resid_cot).astype(jnp.bfloat16)
    return (fresh, normed_b, keyval_cot, gain_cot)

def reference(saved, cot_in, weights, gains, lengths, segments):
    records = {}
    finals = [[None] * N_FSDP for section in range(N_PIPE)]
    for member in range(N_FSDP):
        for item in range(N_PIPE):
            carried = cot_in[item, member]
            for tick in range(TICKS):
                section = (item - tick) % N_PIPE
                layer = item % 2 * N_PIPE + item - tick
                if layer >= 0:
                    stretch = layer // N_PIPE
                    carried, normed_b, keyval_cot, gain_cot = layer_back(saved[section, member, tick], carried, gains[stretch, section], weights[stretch, section], lengths[item, member], segments[item, member])
                    entry_key = (stretch, section, member)
                    if entry_key in records:
                        records[entry_key].append((normed_b, keyval_cot, gain_cot))
                    else:
                        records[entry_key] = [(normed_b, keyval_cot, gain_cot)]
            finals[(item - TICKS + 1) % N_PIPE][member] = carried
    cot_out = jnp.stack([jnp.stack(row) for row in finals])
    kv_stretches = []
    gain_stretches = []
    for stretch in range(2):
        kv_sections = []
        gain_sections = []
        for section in range(N_PIPE):
            kv_total = jnp.zeros((D, KVW), jnp.float32)
            gain_total = jnp.zeros((D,), jnp.float32)
            for member in range(N_FSDP):
                entry_key = (stretch, section, member)
                entries = records[entry_key] if entry_key in records else []
                if entries:
                    normed_all = jnp.concatenate([entry[0] for entry in entries], axis=0)
                    cot_all = jnp.concatenate([entry[1] for entry in entries], axis=0)
                    kv_part = jnp.dot(normed_all.T, cot_all, preferred_element_type=jnp.float32)
                    gain_part = entries[0][2]
                    for entry in entries[1:]:
                        gain_part = gain_part + entry[2]
                    kv_total = kv_total + lax.optimization_barrier(kv_part.astype(jnp.bfloat16)).astype(jnp.float32)
                    gain_total = gain_total + lax.optimization_barrier(gain_part.astype(jnp.bfloat16)).astype(jnp.float32)
            kv_sections.append(kv_total.astype(jnp.bfloat16))
            gain_sections.append(gain_total.astype(jnp.bfloat16))
        kv_stretches.append(jnp.stack(kv_sections))
        gain_stretches.append(jnp.stack(gain_sections))
    return (cot_out, jnp.stack(kv_stretches), jnp.stack(gain_stretches))
```

```python
import functools

import jax
import jax.numpy as jnp
from jax import lax
from jax.experimental import pallas as pl
from jax.experimental.pallas import tpu as pltpu
from jax.sharding import PartitionSpec as P

HEAD_SIZE = 128
PLACES = 4
TICKS = 3
EPS = 1e-05
MESH = pl.DeviceIdType.MESH
LIMIT = 56 * 1024 * 1024
F32 = jnp.float32
B16 = jnp.bfloat16
ACROSS = (((1,), (1,)), ((), ()))
DOWN = (((0,), (0,)), ((), ()))
PLAIN = (((1,), (0,)), ((), ()))


def dot(left, right, dims):
    return lax.dot_general(left, right, dims, preferred_element_type=F32)


def remote(src, dst, send, recv, **where):
    return pltpu.make_async_remote_copy(
        src_ref=src,
        dst_ref=dst,
        send_sem=send,
        recv_sem=recv,
        device_id=where,
        device_id_type=MESH,
    )


def each(low, high, step):
    def one(i, _):
        step(i)
        return 0

    lax.fori_loop(low, high, one, 0)


def relay_kernel(
    n, sections,
    saved, cot, w, gains, lengths, segments,
    out, grad, gain_out,
    xs, xin, qb, qh, cotb, metab, gb, w2, parts, far, ends, kvin, own, kvb,
    kcb, statb, qcb, newc, acc, gacc, gsum, gin,
    x_s, x_r, c_s, c_r, m_s, m_r, g_s, g_r, w_s, w_r, l_s, re_s, re_r, rk_s, rk_r,
    ag_s, ag_r, st_s, st_r, qh_s, qh_r, kl_s, kl_r, pp_s, pp_r, co_s, co_r, gg_s, gg_r,
):
    me = lax.axis_index("fsdp")
    section = lax.axis_index("pipe")
    lanes = n // PLACES
    place, lane = lax.div(me, lanes), lax.rem(me, lanes)
    rows, model = cot.shape
    wide = model // PLACES
    width = w.shape[1]
    half = w.shape[2] // 2
    members = PLACES * rows
    partner = place + 1 - 2 * lax.rem(place, 2)
    upper = lax.div(place, 2)
    is_mid = lax.rem(lax.rem(place, 2) + upper, 2)
    far_mid, far_end = 2 - upper, 3 - 3 * upper
    dests = (lax.rem(place + 2, PLACES), PLACES - 1 - place, partner, place)
    below = lax.rem(section + sections - 1, sections)
    above = lax.rem(section + 1, sections)

    def layer_of(tick):
        item = lax.rem(section + tick, sections)
        return item, lax.rem(item, 2) * sections + item - tick

    def stretch_of(tick):
        return lax.div(jnp.maximum(layer_of(tick)[1], 0), sections)

    first = stretch_of(0)
    second = 1 - first

    def at_place(other):
        return other * lanes + lane

    def at_lane(j):
        return place * lanes + lax.rem(lane + j, lanes)

    def cols(start, size):
        return pl.ds(pl.multiple_of(start, size), size)

    barrier = pltpu.get_barrier_semaphore()

    def greet(**where):
        pl.semaphore_signal(barrier, inc=1, device_id=where, device_id_type=MESH)

    each(1, PLACES, lambda k: greet(fsdp=at_place(lax.rem(place + k, PLACES))))
    each(1, lanes, lambda j: greet(fsdp=at_lane(j)))
    greet(pipe=below)
    greet(pipe=above)

    def own_w(i, stretch):
        mine = cols(lane * width, width)
        return pltpu.make_async_copy(w.at[stretch], w2.at[stretch, mine], l_s.at[i])

    own_w(0, first).start()
    own_w(1, second).start()

    def normalize(tick):
        x = saved[tick].astype(F32)
        factor = lax.rsqrt(jnp.mean(x * x, axis=-1, keepdims=True) + EPS)
        xs[tick] = (x * factor).astype(B16)
        item, _ = layer_of(tick)
        turned = jnp.transpose(jnp.broadcast_to(factor, (rows, HEAD_SIZE)))[0:1]
        doc = segments[pl.ds(item, 1), :].astype(F32)
        used = lengths[pl.ds(item, 1), :].astype(F32)
        metab[place, tick] = jnp.concatenate(
            [
                jnp.concatenate([turned, turned], axis=1),
                jnp.concatenate([doc, doc], axis=1),
                jnp.broadcast_to(used, (1, HEAD_SIZE)),
                jnp.zeros((5, HEAD_SIZE), F32),
            ],
            axis=0,
        )

    normalize(0)
    gb[lane] = gains[...].astype(F32)
    pl.semaphore_wait(barrier, PLACES - 1 + lanes - 1 + 2)

    def x_copy(tick, k):
        to = lax.rem(place + k, PLACES)
        return remote(
            xs.at[tick, :, cols(to * wide, wide)], xin.at[tick, place],
            x_s.at[tick, k], x_r.at[tick, k], fsdp=at_place(to),
        )

    def cot_copy(k):
        to = lax.rem(place + k, PLACES)
        return remote(
            cot.at[:, cols(to * wide, wide)], cotb.at[0, place],
            c_s.at[k], c_r.at[k], fsdp=at_place(to),
        )

    def meta_copy(tick, k):
        to = lax.rem(place + k, PLACES)
        return remote(
            metab.at[place, tick], metab.at[place, tick],
            m_s.at[tick, k], m_r.at[tick, k], fsdp=at_place(to),
        )

    def gain_copy(j):
        return remote(gb.at[lane], gb.at[lane], g_s.at[j], g_r.at[j], fsdp=at_lane(j))

    def w_copy(i, k, side, j):
        stretch = (first, second)[i]
        here = cols(dests[k] * HEAD_SIZE + side * half, HEAD_SIZE)
        return remote(
            w.at[stretch, :, here], w2.at[stretch, cols(lane * width, width), here],
            w_s.at[i, k, side, j], w_r.at[i, k, side, j], fsdp=at_lane(j),
        )

    def send_w(i):
        for k in range(4):
            for side in range(2):
                each(1, lanes, lambda j: w_copy(i, k, side, j).start())

    each(1, lanes, lambda j: gain_copy(j).start())
    each(1, PLACES, lambda k: x_copy(0, k).start())
    send_w(0)
    each(1, PLACES, lambda k: meta_copy(0, k).start())
    each(1, PLACES, lambda k: cot_copy(k).start())
    send_w(1)

    xin[0, place] = xs[0, :, cols(place * wide, wide)]
    cotb[0, place] = cot[:, cols(place * wide, wide)]
    for tick in (1, 2):
        normalize(tick)
        each(1, PLACES, lambda k: meta_copy(tick, k).start())
        xin[tick, place] = xs[tick, :, cols(place * wide, wide)]
    acc[...] = jnp.zeros_like(acc)
    gacc[...] = jnp.zeros_like(gacc)
    each(1, lanes, lambda j: gain_copy(j).wait_recv())

    def gain_of(tick):
        stretch = stretch_of(tick)
        return jnp.concatenate(
            [gb[i, pl.ds(stretch, 1), :] for i in range(lanes)], axis=1
        )

    def q_copy(tick, j):
        to = lax.rem(lane + j, lanes)
        return remote(
            qb.at[tick, :, cols(to * width, width)], qh.at[lane, tick],
            qh_s.at[tick, j], qh_r.at[tick, j], fsdp=at_lane(j),
        )

    def end_copy(tick, k):
        return remote(
            parts.at[tick, k], ends.at[tick, k],
            re_s.at[tick, k], re_r.at[tick, k], fsdp=at_place(partner),
        )

    def partner_copy(tick):
        return remote(
            parts.at[tick, 2], kvin.at[tick, 0],
            rk_s.at[tick, 2], rk_r.at[tick, 0], fsdp=at_place(partner),
        )

    def far_copy(tick, k):
        return remote(
            parts.at[tick, k], kvin.at[tick, 1],
            rk_s.at[tick, k], rk_r.at[tick, 1], fsdp=at_place(dests[k]),
        )

    def forward(tick):
        stretch = stretch_of(tick)
        each(1, PLACES, lambda k: x_copy(tick, k).wait_recv())
        q = (xin[tick].reshape(members, wide).astype(F32) * gain_of(tick)).astype(B16)
        qb[tick] = q
        if tick < 2:
            own_w(tick, (first, second)[tick]).wait()
        for k in range(4):
            if tick < 2:
                for side in range(2):
                    each(1, lanes, lambda j: w_copy(tick, k, side, j).wait_recv())
            at = [cols(dests[k] * HEAD_SIZE + side * half, HEAD_SIZE) for side in range(2)]
            right = jnp.concatenate([w2[stretch, :, a] for a in at], axis=1)
            part = dot(qb[tick], right, PLAIN)
            if k < 2:
                far[k] = part

                @pl.when(is_mid == 0)
                def _():
                    parts[tick, k] = far[k].astype(B16)
                    end_copy(tick, k).start()

            elif k == 2:
                parts[tick, 2] = part.astype(B16)
                partner_copy(tick).start()
            else:
                own[tick] = part

        @pl.when(is_mid == 1)
        def _():
            for k in range(2):
                end_copy(tick, 1 - k).wait_recv()
                parts[tick, k] = (far[k] + ends[tick, 1 - k].astype(F32)).astype(B16)
                far_copy(tick, k).start()

    def gather_kv(tick):
        partner_copy(tick).wait_recv()
        far_copy(tick, 0).wait_recv()
        total = own[tick] + kvin[tick, 0].astype(F32) + kvin[tick, 1].astype(F32)
        kvb[tick] = total.astype(B16).reshape(PLACES, rows, 2 * HEAD_SIZE)

    def pipe_copy(tick, m):
        return remote(
            newc.at[tick, m], cotb.at[tick + 1, m],
            pp_s.at[tick, m], pp_r.at[tick, m], pipe=below,
        )

    def near_copies(tick, m, which=(0, 1)):
        chunk, stat = kcb.at[lane, tick, place, m], statb.at[tick, place, m]
        copies = []
        for i in which:
            to, slot = ((partner, 0), (far_mid, 2 - is_mid))[i]
            for ref, send, recv in ((chunk, ag_s, ag_r), (stat, st_s, st_r)):
                copies.append(
                    remote(ref, ref, send.at[tick, m, i], recv.at[tick, m, slot],
                           fsdp=at_place(to))
                )
        return copies

    def pass_copies(tick, m, slot):
        source = (far_mid, far_end)[slot - 1]
        chunk, stat = kcb.at[lane, tick, source, m], statb.at[tick, source, m]
        return [
            remote(chunk, chunk, ag_s.at[tick, m, 1 + slot], ag_r.at[tick, m, slot],
                   fsdp=at_place(partner)),
            remote(stat, stat, st_s.at[tick, m, 1 + slot], st_r.at[tick, m, slot],
                   fsdp=at_place(partner)),
        ]

    def pass_on(tick, m):
        @pl.when(is_mid == 1)
        def _():
            for slot in (1, 2):
                for copy in pass_copies(tick, m, slot):
                    copy.wait_recv()
                    copy.start()

    def heads(value):
        return jnp.concatenate(
            [
                value[:, i * HEAD_SIZE : (i + 1) * HEAD_SIZE]
                for i in range(wide // HEAD_SIZE)
            ],
            axis=0,
        )

    groups = wide // HEAD_SIZE
    scale = HEAD_SIZE ** (-0.5)

    def attend(tick, m):
        if tick:
            pipe_copy(tick - 1, m).wait_recv()
        item, layer = layer_of(tick)
        active = jnp.where(layer >= 0, 1.0, 0.0).astype(F32)
        query = heads(qb[tick, pl.ds(pl.multiple_of(m * rows, rows), rows), :])
        pulled = heads(cotb[tick, m])
        keys = kvb[tick, m, :, :HEAD_SIZE]
        values = kvb[tick, m, :, HEAD_SIZE:]
        meta = metab[m, tick]
        turned = jnp.transpose(meta)

        def across(row):
            return jnp.concatenate([meta[row : row + 1]] * (groups * rows // HEAD_SIZE), axis=1)

        shape = (rows, groups * rows)
        spot = lax.broadcasted_iota(jnp.int32, shape, 0)
        seer = lax.rem(lax.broadcasted_iota(jnp.int32, shape, 1), rows)
        key_spot = lax.broadcasted_iota(jnp.int32, (rows, 1), 0).astype(F32)
        doc = jnp.where(key_spot < turned[:rows, 2:3], turned[:rows, 1:2], -1.0)
        seen = ((doc == across(1)) & (spot <= seer)) | (spot == seer)
        row_spot = seer[0:1].astype(F32)
        valid = jnp.where(row_spot < across(2) * active, 1.0, 0.0)
        raw = dot(keys, query, ACROSS)
        scores = jnp.where(seen, raw * scale, -1e30)
        expo = jnp.exp(scores - jnp.max(scores, axis=0, keepdims=True))
        probs = expo / jnp.sum(expo, axis=0, keepdims=True)
        prob_cot = dot(values, pulled, ACROSS).astype(B16).astype(F32) * valid
        inner = jnp.sum(probs * prob_cot, axis=0, keepdims=True)
        score_cot = jnp.where(seen, probs * (prob_cot - inner), 0.0) * scale
        score_b = score_cot.astype(B16)
        query_cot = dot(score_b, keys, DOWN)
        for i in range(groups):
            qcb[m, :, i * HEAD_SIZE : (i + 1) * HEAD_SIZE] = query_cot[
                i * rows : (i + 1) * rows
            ].astype(B16)
        key_cot = dot(score_b, query, PLAIN).astype(B16)
        value_cot = dot((probs * valid).astype(B16), pulled, PLAIN).astype(B16)
        kcb[lane, tick, place, m, :, :HEAD_SIZE] = key_cot
        kcb[lane, tick, place, m, :, HEAD_SIZE:] = value_cot
        line = jnp.sum(score_cot * raw, axis=0, keepdims=True)
        while line.shape[1] > HEAD_SIZE:
            cut = line.shape[1] // 2
            line = line[:, :cut] + line[:, cut:]
        line = line + pltpu.roll(line, rows, 1)
        both = keys.astype(F32) * key_cot.astype(F32) + values.astype(F32) * value_cot.astype(F32)
        high = both.astype(B16)
        low = (both - high.astype(F32)).astype(B16)
        ones = jnp.ones((8, HEAD_SIZE), B16)
        flat = dot(ones, high, ACROSS) + dot(ones, low, ACROSS)
        statb[tick, place, m] = jnp.concatenate([flat, flat], axis=1) + line
        for copy in near_copies(tick, m):
            copy.start()

    def lane_copy(tick, m, j):
        chunk = kcb.at[lane, tick, :, m]
        return remote(chunk, chunk, kl_s.at[tick, m, j], kl_r.at[tick, m, j], fsdp=at_lane(j))

    def out_copy(m):
        return remote(
            newc.at[TICKS - 1, m], out.at[:, cols(place * wide, wide)],
            co_s.at[m], co_r.at[place], fsdp=at_place(m),
        )

    def settle(tick, m):
        stretch = stretch_of(tick)
        for copy in near_copies(tick, m, (0,)):
            copy.wait_recv()

        @pl.when(is_mid == 0)
        def _():
            for slot in (1, 2):
                for copy in pass_copies(tick, m, slot):
                    copy.wait_recv()

        each(1, lanes, lambda j: lane_copy(tick, m, j).start())
        kc = jnp.concatenate(
            [
                kcb[lane, tick, d, m, :, side * HEAD_SIZE : (side + 1) * HEAD_SIZE]
                for side in range(2)
                for d in range(PLACES)
            ],
            axis=1,
        )
        total = qcb[m].astype(F32) + dot(kc, w2[stretch], ACROSS)
        stat = statb[tick, 0, m]
        for d in range(1, PLACES):
            stat = stat + statb[tick, d, m]
        mean = jnp.transpose(stat)[:rows, 0:1] * (1.0 / model)
        factor = jnp.transpose(metab[m, tick])[:rows, 0:1]
        xhat = xin[tick, m].astype(F32)
        gain = gain_of(tick)
        gacc[stretch] += jnp.sum((xhat * total).reshape(rows // 8, 8, wide), axis=0)
        x_cot = factor * (gain * total - xhat * mean)
        fresh = (cotb[tick, m].astype(F32) + x_cot).astype(B16)
        newc[tick, m] = fresh
        if tick < TICKS - 1:
            pipe_copy(tick, m).start()
        else:

            @pl.when(m == place)
            def _():
                out[:, cols(place * wide, wide)] = newc[tick, m]

            @pl.when(m != place)
            def _():
                out_copy(m).start()

    def weigh(tick):
        stretch = stretch_of(tick)
        qh[lane, tick] = qb[tick, :, cols(lane * width, width)]
        each(1, lanes, lambda j: q_copy(tick, j).wait_recv())
        each(0, PLACES, lambda m: each(1, lanes, lambda j: lane_copy(tick, m, j).wait_recv()))

        def one(d):
            total = acc[stretch, d]
            for i in range(lanes):
                right = kcb[i, tick, d].reshape(members, 2 * HEAD_SIZE)
                total = total + dot(qh[i, tick], right, DOWN)
            acc[stretch, d] = total

        each(0, PLACES, one)

    forward(0)
    each(1, PLACES, lambda k: x_copy(1, k).start())
    each(1, PLACES, lambda k: meta_copy(0, k).wait_recv())
    each(1, PLACES, lambda k: cot_copy(k).wait_recv())
    gather_kv(0)
    for tick in range(TICKS):

        def step(m):
            attend(tick, m)

            @pl.when(m > 0)
            def _():
                pass_on(tick, m - 1)

        each(0, PLACES, step)
        pass_on(tick, PLACES - 1)
        each(1, lanes, lambda j: q_copy(tick, j).start())
        if tick == 0:
            each(1, PLACES, lambda k: x_copy(2, k).start())
        each(0, PLACES, lambda m: settle(tick, m))
        if tick < TICKS - 1:
            forward(tick + 1)
            if tick:
                weigh(tick - 1)
            each(1, PLACES, lambda k: meta_copy(tick + 1, k).wait_recv())
            gather_kv(tick + 1)

    gain_sum = jnp.sum(gacc[...], axis=1)
    for i in range(lanes):
        gsum[i] = gain_sum[:, i * width : (i + 1) * width]

    def sum_copy(j):
        to = lax.rem(lane + j, lanes)
        return remote(gsum.at[to], gin.at[lane], gg_s.at[j], gg_r.at[j], fsdp=at_lane(j))

    each(1, lanes, lambda j: sum_copy(j).start())
    gin[lane] = gsum[lane]
    weigh(TICKS - 2)
    weigh(TICKS - 1)
    for d in range(PLACES):
        for side in range(2):
            start = d * HEAD_SIZE + side * half
            grad[:, :, start : start + HEAD_SIZE] = acc[
                :, d, :, side * HEAD_SIZE : (side + 1) * HEAD_SIZE
            ].astype(B16)
    each(1, lanes, lambda j: sum_copy(j).wait())
    gain_out[...] = jnp.sum(gin[...], axis=0).astype(B16)

    def out_wait(k):
        to = lax.rem(place + k, PLACES)
        out_copy(to).wait_send()
        remote(
            newc.at[TICKS - 1, to], out.at[:, cols(to * wide, wide)],
            co_s.at[to], co_r.at[to], fsdp=at_place(to),
        ).wait_recv()

    each(1, PLACES, out_wait)
    each(1, PLACES, lambda k: cot_copy(k).wait_send())
    each(1, lanes, lambda j: gain_copy(j).wait_send())
    for i in range(2):
        for k in range(4):
            for side in range(2):
                each(1, lanes, lambda j: w_copy(i, k, side, j).wait_send())
    for tick in range(TICKS):
        each(1, PLACES, lambda k: x_copy(tick, k).wait_send())
        each(1, PLACES, lambda k: meta_copy(tick, k).wait_send())
        each(1, lanes, lambda j: q_copy(tick, j).wait_send())
        partner_copy(tick).wait_send()

        def finish(m):
            for copy in near_copies(tick, m):
                copy.wait_send()
            each(1, lanes, lambda j: lane_copy(tick, m, j).wait_send())
            if tick < TICKS - 1:
                pipe_copy(tick, m).wait_send()

            @pl.when(is_mid == 1)
            def _():
                for slot in (1, 2):
                    for copy in pass_copies(tick, m, slot):
                        copy.wait_send()

        each(0, PLACES, finish)

        @pl.when(is_mid == 1)
        def _():
            for k in range(2):
                far_copy(tick, k).wait_send()

        @pl.when(is_mid == 0)
        def _():
            for k in range(2):
                end_copy(tick, k).wait_send()


def relay(n, sections, saved, cot, w, gains, lengths, segments):
    ticks, rows, model = saved.shape
    width, kvw = w.shape[1:]
    lanes = n // PLACES
    wide = model // PLACES
    members = PLACES * rows
    pair = 2 * HEAD_SIZE
    vmem = pl.BlockSpec(memory_space=pltpu.VMEM)
    dma = pltpu.SemaphoreType.DMA
    return pl.pallas_call(
        functools.partial(relay_kernel, n, sections),
        out_shape=(
            jax.ShapeDtypeStruct((rows, model), B16),
            jax.ShapeDtypeStruct(w.shape, B16),
            jax.ShapeDtypeStruct(gains.shape, B16),
        ),
        in_specs=[vmem, vmem, pl.BlockSpec(memory_space=pl.ANY), vmem, vmem, vmem],
        out_specs=(vmem,) * 3,
        scratch_shapes=[
            pltpu.VMEM((ticks, rows, model), B16),
            pltpu.VMEM((ticks, PLACES, rows, wide), B16),
            pltpu.VMEM((ticks, members, wide), B16),
            pltpu.VMEM((lanes, ticks, members, width), B16),
            pltpu.VMEM((ticks, PLACES, rows, wide), B16),
            pltpu.VMEM((PLACES, ticks, 8, HEAD_SIZE), F32),
            pltpu.VMEM((lanes, 2, width), F32),
            pltpu.VMEM((2, lanes * width, kvw), B16),
            pltpu.VMEM((ticks, 3, members, pair), B16),
            pltpu.VMEM((2, members, pair), F32),
            pltpu.VMEM((ticks, 2, members, pair), B16),
            pltpu.VMEM((ticks, 2, members, pair), B16),
            pltpu.VMEM((ticks, members, pair), F32),
            pltpu.VMEM((ticks, PLACES, rows, pair), B16),
            pltpu.VMEM((lanes, ticks, PLACES, PLACES, rows, pair), B16),
            pltpu.VMEM((ticks, PLACES, PLACES, 8, HEAD_SIZE), F32),
            pltpu.VMEM((PLACES, rows, wide), B16),
            pltpu.VMEM((ticks, PLACES, rows, wide), B16),
            pltpu.VMEM((2, PLACES, width, pair), F32),
            pltpu.VMEM((2, 8, wide), F32),
            pltpu.VMEM((lanes, 2, width), F32),
            pltpu.VMEM((lanes, 2, width), F32),
        ]
        + [dma((ticks, PLACES))] * 2
        + [dma((PLACES,))] * 2
        + [dma((ticks, PLACES))] * 2
        + [dma((lanes,))] * 2
        + [dma((2, 4, 2, lanes))] * 2
        + [dma((2,))]
        + [dma((ticks, 2))] * 2
        + [dma((ticks, 3)), dma((ticks, 2))]
        + [dma((ticks, PLACES, 4)), dma((ticks, PLACES, 3))]
        + [dma((ticks, PLACES, 4)), dma((ticks, PLACES, 3))]
        + [dma((ticks, lanes))] * 2
        + [dma((ticks, PLACES, lanes))] * 2
        + [dma((ticks, PLACES))] * 2
        + [dma((PLACES,))] * 2
        + [dma((lanes,))] * 2,
        compiler_params=pltpu.CompilerParams(
            collective_id=0, has_side_effects=True, vmem_limit_bytes=LIMIT
        ),
    )(saved, cot, w, gains, lengths, segments)


def body(saved, cot_in, weights, gains, lengths, segments):
    out, grad_kv, grad_gain = relay(
        lax.axis_size("fsdp"), lax.axis_size("pipe"),
        saved[0, 0], cot_in[0, 0], weights[:, 0], gains[:, 0], lengths, segments[:, 0],
    )
    return out[None, None], grad_kv[:, None], grad_gain[:, None]


def solution(mesh):
    in_specs = (
        P("pipe", "fsdp", None, None, None),
        P("pipe", "fsdp", None, None),
        P(None, "pipe", "fsdp", None),
        P(None, "pipe", "fsdp"),
        P(None, "fsdp"),
        P(None, "fsdp", None),
    )
    out_specs = (
        P("pipe", "fsdp", None, None),
        P(None, "pipe", "fsdp", None),
        P(None, "pipe", "fsdp"),
    )
    return jax.shard_map(body, mesh=mesh, in_specs=in_specs, out_specs=out_specs, check_vma=False)
```

```python
import functools

import jax
import jax.numpy as jnp
from jax import lax
from jax.experimental import pallas as pl
from jax.experimental.pallas import tpu as pltpu
from jax.sharding import PartitionSpec as P

HEAD_SIZE = 128
PLACES = 4
TICKS = 3
EPS = 1e-05
MESH = pl.DeviceIdType.MESH
F32 = jnp.float32
B16 = jnp.bfloat16
ACROSS = (((1,), (1,)), ((), ()))
DOWN = (((0,), (0,)), ((), ()))
PLAIN = (((1,), (0,)), ((), ()))


def dot(left, right, dims):
    return lax.dot_general(left, right, dims, preferred_element_type=F32)


def remote(src, dst, send, recv, **where):
    return pltpu.make_async_remote_copy(
        src_ref=src,
        dst_ref=dst,
        send_sem=send,
        recv_sem=recv,
        device_id=where,
        device_id_type=MESH,
    )


def each(low, high, step):
    def one(i, _):
        step(i)
        return 0

    lax.fori_loop(low, high, one, 0)


def relay_kernel(
    n, sections,
    saved, cot, w, gains, lengths, segments,
    out, grad, gain_out,
    xs, xin, qb, qh, cotb, metab, gb, w2, parts, far, ends, kvin, own, kvb,
    kcb, statb, qcb, newc, acc, gacc, gsum, gin,
    x_s, x_r, c_s, c_r, m_s, m_r, g_s, g_r, w_s, w_r, l_s, re_s, re_r, rk_s, rk_r,
    ag_s, ag_r, st_s, st_r, qh_s, qh_r, kl_s, kl_r, pp_s, pp_r, co_s, co_r, gg_s, gg_r,
):
    me = lax.axis_index("fsdp")
    section = lax.axis_index("pipe")
    lanes = n // PLACES
    place, lane = lax.div(me, lanes), lax.rem(me, lanes)
    rows, model = cot.shape
    wide = model // PLACES
    width = w.shape[1]
    half = w.shape[2] // 2
    members = PLACES * rows
    partner = place + 1 - 2 * lax.rem(place, 2)
    upper = lax.div(place, 2)
    is_mid = lax.rem(lax.rem(place, 2) + upper, 2)
    far_mid, far_end = 2 - upper, 3 - 3 * upper
    dests = (lax.rem(place + 2, PLACES), PLACES - 1 - place, partner, place)
    below = lax.rem(section + sections - 1, sections)
    above = lax.rem(section + 1, sections)

    def layer_of(tick):
        item = lax.rem(section + tick, sections)
        return item, lax.rem(item, 2) * sections + item - tick

    def stretch_of(tick):
        return lax.div(jnp.maximum(layer_of(tick)[1], 0), sections)

    first = stretch_of(0)
    second = 1 - first

    def at_place(other):
        return other * lanes + lane

    def at_lane(j):
        return place * lanes + lax.rem(lane + j, lanes)

    def cols(start, size):
        return pl.ds(pl.multiple_of(start, size), size)

    barrier = pltpu.get_barrier_semaphore()

    def greet(**where):
        pl.semaphore_signal(barrier, inc=1, device_id=where, device_id_type=MESH)

    each(1, PLACES, lambda k: greet(fsdp=at_place(lax.rem(place + k, PLACES))))
    each(1, lanes, lambda j: greet(fsdp=at_lane(j)))
    greet(pipe=below)
    greet(pipe=above)

    def own_w(i, stretch):
        mine = cols(lane * width, width)
        return pltpu.make_async_copy(w.at[stretch], w2.at[stretch, mine], l_s.at[i])

    own_w(0, first).start()
    own_w(1, second).start()

    def normalize(tick):
        x = saved[tick].astype(F32)
        factor = lax.rsqrt(jnp.mean(x * x, axis=-1, keepdims=True) + EPS)
        xs[tick] = (x * factor).astype(B16)
        item, _ = layer_of(tick)
        turned = jnp.transpose(jnp.broadcast_to(factor, (rows, HEAD_SIZE)))[0:1]
        doc = segments[pl.ds(item, 1), :].astype(F32)
        at = lax.broadcasted_iota(jnp.int32, lengths.shape, 1)
        used = jnp.sum(jnp.where(at == item, lengths[...].astype(F32), 0.0), axis=1, keepdims=True)
        metab[place, tick] = jnp.concatenate(
            [
                jnp.concatenate([turned, turned], axis=1),
                jnp.concatenate([doc, doc], axis=1),
                jnp.broadcast_to(used, (1, HEAD_SIZE)),
                jnp.zeros((5, HEAD_SIZE), F32),
            ],
            axis=0,
        )

    normalize(0)
    gb[lane] = gains[...].astype(F32)
    pl.semaphore_wait(barrier, PLACES - 1 + lanes - 1 + 2)

    def x_copy(tick, k):
        to = lax.rem(place + k, PLACES)
        return remote(
            xs.at[tick, :, cols(to * wide, wide)], xin.at[tick, place],
            x_s.at[tick, k], x_r.at[tick, k], fsdp=at_place(to),
        )

    def cot_copy(k):
        to = lax.rem(place + k, PLACES)
        return remote(
            cot.at[:, cols(to * wide, wide)], cotb.at[0, place],
            c_s.at[k], c_r.at[k], fsdp=at_place(to),
        )

    def meta_copy(tick, k):
        to = lax.rem(place + k, PLACES)
        return remote(
            metab.at[place, tick], metab.at[place, tick],
            m_s.at[tick, k], m_r.at[tick, k], fsdp=at_place(to),
        )

    def gain_copy(j):
        return remote(gb.at[lane], gb.at[lane], g_s.at[j], g_r.at[j], fsdp=at_lane(j))

    def w_copy(i, k, side, j):
        stretch = (first, second)[i]
        here = cols(dests[k] * HEAD_SIZE + side * half, HEAD_SIZE)
        return remote(
            w.at[stretch, :, here], w2.at[stretch, cols(lane * width, width), here],
            w_s.at[i, k, side, j], w_r.at[i, k, side, j], fsdp=at_lane(j),
        )

    def send_w(i):
        for k in range(4):
            for side in range(2):
                each(1, lanes, lambda j: w_copy(i, k, side, j).start())

    each(1, lanes, lambda j: gain_copy(j).start())
    each(1, PLACES, lambda k: x_copy(0, k).start())
    send_w(0)
    each(1, PLACES, lambda k: meta_copy(0, k).start())
    each(1, PLACES, lambda k: cot_copy(k).start())
    send_w(1)

    xin[0, place] = xs[0, :, cols(place * wide, wide)]
    cotb[0, place] = cot[:, cols(place * wide, wide)]
    for tick in (1, 2):
        normalize(tick)
        each(1, PLACES, lambda k: meta_copy(tick, k).start())
        xin[tick, place] = xs[tick, :, cols(place * wide, wide)]
    acc[...] = jnp.zeros_like(acc)
    gacc[...] = jnp.zeros_like(gacc)
    each(1, lanes, lambda j: gain_copy(j).wait_recv())

    def gain_of(tick):
        stretch = stretch_of(tick)
        return jnp.concatenate(
            [gb[i, pl.ds(stretch, 1), :] for i in range(lanes)], axis=1
        )

    def q_copy(tick, j):
        to = lax.rem(lane + j, lanes)
        return remote(
            qb.at[tick, :, cols(to * width, width)], qh.at[lane, tick],
            qh_s.at[tick, j], qh_r.at[tick, j], fsdp=at_lane(j),
        )

    def end_copy(tick, k):
        return remote(
            parts.at[tick, k], ends.at[tick, k],
            re_s.at[tick, k], re_r.at[tick, k], fsdp=at_place(partner),
        )

    def partner_copy(tick):
        return remote(
            parts.at[tick, 2], kvin.at[tick, 0],
            rk_s.at[tick, 2], rk_r.at[tick, 0], fsdp=at_place(partner),
        )

    def far_copy(tick, k):
        return remote(
            parts.at[tick, k], kvin.at[tick, 1],
            rk_s.at[tick, k], rk_r.at[tick, 1], fsdp=at_place(dests[k]),
        )

    def forward(tick):
        stretch = stretch_of(tick)
        each(1, PLACES, lambda k: x_copy(tick, k).wait_recv())
        q = (xin[tick].reshape(members, wide).astype(F32) * gain_of(tick)).astype(B16)
        qb[tick] = q
        if tick < 2:
            own_w(tick, (first, second)[tick]).wait()
        for k in range(4):
            if tick < 2:
                for side in range(2):
                    each(1, lanes, lambda j: w_copy(tick, k, side, j).wait_recv())
            at = [cols(dests[k] * HEAD_SIZE + side * half, HEAD_SIZE) for side in range(2)]
            right = jnp.concatenate([w2[stretch, :, a] for a in at], axis=1)
            part = dot(qb[tick], right, PLAIN)
            if k < 2:
                far[k] = part

                @pl.when(is_mid == 0)
                def _():
                    parts[tick, k] = far[k].astype(B16)
                    end_copy(tick, k).start()

            elif k == 2:
                parts[tick, 2] = part.astype(B16)
                partner_copy(tick).start()
            else:
                own[tick] = part

    def combine(tick):
        @pl.when(is_mid == 1)
        def _():
            for k in range(2):
                end_copy(tick, 1 - k).wait_recv()
                parts[tick, k] = (far[k] + ends[tick, 1 - k].astype(F32)).astype(B16)
                far_copy(tick, k).start()

    def gather_kv(tick):
        partner_copy(tick).wait_recv()
        far_copy(tick, 0).wait_recv()
        total = own[tick] + kvin[tick, 0].astype(F32) + kvin[tick, 1].astype(F32)
        kvb[tick] = total.astype(B16).reshape(PLACES, rows, 2 * HEAD_SIZE)

    def pipe_copy(tick, m):
        return remote(
            newc.at[tick, m], cotb.at[tick + 1, m],
            pp_s.at[tick, m], pp_r.at[tick, m], pipe=below,
        )

    def near_copies(tick, m, which=(0, 1)):
        chunk, stat = kcb.at[lane, tick, place, m], statb.at[tick, place, m]
        copies = []
        for i in which:
            to, slot = ((partner, 0), (far_mid, 2 - is_mid))[i]
            for ref, send, recv in ((chunk, ag_s, ag_r), (stat, st_s, st_r)):
                copies.append(
                    remote(ref, ref, send.at[tick, m, i], recv.at[tick, m, slot],
                           fsdp=at_place(to))
                )
        return copies

    def pass_copies(tick, m, slot):
        source = (far_mid, far_end)[slot - 1]
        chunk, stat = kcb.at[lane, tick, source, m], statb.at[tick, source, m]
        return [
            remote(chunk, chunk, ag_s.at[tick, m, 1 + slot], ag_r.at[tick, m, slot],
                   fsdp=at_place(partner)),
            remote(stat, stat, st_s.at[tick, m, 1 + slot], st_r.at[tick, m, slot],
                   fsdp=at_place(partner)),
        ]

    def pass_on(tick, m):
        @pl.when(is_mid == 1)
        def _():
            for slot in (1, 2):
                for copy in pass_copies(tick, m, slot):
                    copy.wait_recv()
                    copy.start()

    def heads(value):
        return jnp.concatenate(
            [
                value[:, i * HEAD_SIZE : (i + 1) * HEAD_SIZE]
                for i in range(wide // HEAD_SIZE)
            ],
            axis=0,
        )

    groups = wide // HEAD_SIZE
    scale = HEAD_SIZE ** (-0.5)

    def attend(tick, m):
        if tick:
            pipe_copy(tick - 1, m).wait_recv()
        item, layer = layer_of(tick)
        active = jnp.where(layer >= 0, 1.0, 0.0).astype(F32)
        query = heads(qb[tick, pl.ds(pl.multiple_of(m * rows, rows), rows), :])
        pulled = heads(cotb[tick, m])
        keys = kvb[tick, m, :, :HEAD_SIZE]
        values = kvb[tick, m, :, HEAD_SIZE:]
        meta = metab[m, tick]
        turned = jnp.transpose(meta)

        def across(row):
            return jnp.concatenate([meta[row : row + 1]] * (groups * rows // HEAD_SIZE), axis=1)

        shape = (rows, groups * rows)
        spot = lax.broadcasted_iota(jnp.int32, shape, 0)
        seer = lax.rem(lax.broadcasted_iota(jnp.int32, shape, 1), rows)
        key_spot = lax.broadcasted_iota(jnp.int32, (rows, 1), 0).astype(F32)
        doc = jnp.where(key_spot < turned[:rows, 2:3], turned[:rows, 1:2], -1.0)
        seen = ((doc == across(1)) & (spot <= seer)) | (spot == seer)
        row_spot = seer[0:1].astype(F32)
        valid = jnp.where(row_spot < across(2) * active, 1.0, 0.0)
        raw = dot(keys, query, ACROSS)
        scores = jnp.where(seen, raw * scale, -1e30)
        expo = jnp.exp(scores - jnp.max(scores, axis=0, keepdims=True))
        probs = expo / jnp.sum(expo, axis=0, keepdims=True)
        prob_cot = dot(values, pulled, ACROSS).astype(B16).astype(F32) * valid
        inner = jnp.sum(probs * prob_cot, axis=0, keepdims=True)
        score_cot = jnp.where(seen, probs * (prob_cot - inner), 0.0) * scale
        score_b = score_cot.astype(B16)
        query_cot = dot(score_b, keys, DOWN)
        for i in range(groups):
            qcb[m, :, i * HEAD_SIZE : (i + 1) * HEAD_SIZE] = query_cot[
                i * rows : (i + 1) * rows
            ].astype(B16)
        key_cot = dot(score_b, query, PLAIN).astype(B16)
        value_cot = dot((probs * valid).astype(B16), pulled, PLAIN).astype(B16)
        kcb[lane, tick, place, m, :, :HEAD_SIZE] = key_cot
        kcb[lane, tick, place, m, :, HEAD_SIZE:] = value_cot
        line = jnp.sum(score_cot * raw, axis=0, keepdims=True)
        while line.shape[1] > HEAD_SIZE:
            cut = line.shape[1] // 2
            line = line[:, :cut] + line[:, cut:]
        line = line + pltpu.roll(line, rows, 1)
        both = keys.astype(F32) * key_cot.astype(F32) + values.astype(F32) * value_cot.astype(F32)
        high = both.astype(B16)
        low = (both - high.astype(F32)).astype(B16)
        ones = jnp.ones((8, HEAD_SIZE), B16)
        flat = dot(ones, high, ACROSS) + dot(ones, low, ACROSS)
        statb[tick, place, m] = jnp.concatenate([flat, flat], axis=1) + line
        for copy in near_copies(tick, m):
            copy.start()

    def lane_copy(tick, m, j):
        chunk = kcb.at[lane, tick, :, m]
        return remote(chunk, chunk, kl_s.at[tick, m, j], kl_r.at[tick, m, j], fsdp=at_lane(j))

    def out_copy(m):
        return remote(
            newc.at[TICKS - 1, m], out.at[:, cols(place * wide, wide)],
            co_s.at[m], co_r.at[place], fsdp=at_place(m),
        )

    def settle(tick, m):
        stretch = stretch_of(tick)
        for copy in near_copies(tick, m, (0,)):
            copy.wait_recv()

        @pl.when(is_mid == 0)
        def _():
            for slot in (1, 2):
                for copy in pass_copies(tick, m, slot):
                    copy.wait_recv()

        each(1, lanes, lambda j: lane_copy(tick, m, j).start())
        kc = jnp.concatenate(
            [
                kcb[lane, tick, d, m, :, side * HEAD_SIZE : (side + 1) * HEAD_SIZE]
                for side in range(2)
                for d in range(PLACES)
            ],
            axis=1,
        )
        total = qcb[m].astype(F32) + dot(kc, w2[stretch], ACROSS)
        stat = statb[tick, 0, m]
        for d in range(1, PLACES):
            stat = stat + statb[tick, d, m]
        mean = jnp.transpose(stat)[:rows, 0:1] * (1.0 / model)
        factor = jnp.transpose(metab[m, tick])[:rows, 0:1]
        xhat = xin[tick, m].astype(F32)
        gain = gain_of(tick)
        gacc[stretch] += jnp.sum((xhat * total).reshape(rows // 8, 8, wide), axis=0)
        x_cot = factor * (gain * total - xhat * mean)
        fresh = (cotb[tick, m].astype(F32) + x_cot).astype(B16)
        newc[tick, m] = fresh
        if tick < TICKS - 1:
            pipe_copy(tick, m).start()
        else:

            @pl.when(m == place)
            def _():
                out[:, cols(place * wide, wide)] = newc[tick, m]

            @pl.when(m != place)
            def _():
                out_copy(m).start()

    def weigh(tick):
        stretch = stretch_of(tick)
        qh[lane, tick] = qb[tick, :, cols(lane * width, width)]
        each(1, lanes, lambda j: q_copy(tick, j).wait_recv())
        each(0, PLACES, lambda m: each(1, lanes, lambda j: lane_copy(tick, m, j).wait_recv()))

        def one(d):
            total = acc[stretch, d]
            for i in range(lanes):
                right = kcb[i, tick, d].reshape(members, 2 * HEAD_SIZE)
                total = total + dot(qh[i, tick], right, DOWN)
            acc[stretch, d] = total

        each(0, PLACES, one)

    forward(0)
    x_copy(1, 2).start()
    combine(0)
    x_copy(1, 1).start()
    x_copy(1, 3).start()
    each(1, PLACES, lambda k: meta_copy(0, k).wait_recv())
    each(1, PLACES, lambda k: cot_copy(k).wait_recv())
    for tick in range(TICKS):
        gather_kv(tick)
        each(0, PLACES, lambda m: attend(tick, m))
        pass_on(tick, 0)
        if tick < TICKS - 1:
            forward(tick + 1)
        if tick == 0:
            x_copy(2, 2).start()

        def step(m):
            @pl.when(m < PLACES - 1)
            def _():
                pass_on(tick, m + 1)

            settle(tick, m)

        each(0, PLACES, step)
        if tick == 0:
            x_copy(2, 1).start()
            x_copy(2, 3).start()
        each(1, lanes, lambda j: q_copy(tick, j).start())
        if tick < TICKS - 1:
            combine(tick + 1)
            each(1, PLACES, lambda k: meta_copy(tick + 1, k).wait_recv())
            if tick:
                weigh(tick - 1)

    gain_sum = jnp.sum(gacc[...], axis=1)
    for i in range(lanes):
        gsum[i] = gain_sum[:, i * width : (i + 1) * width]

    def sum_copy(j):
        to = lax.rem(lane + j, lanes)
        return remote(gsum.at[to], gin.at[lane], gg_s.at[j], gg_r.at[j], fsdp=at_lane(j))

    each(1, lanes, lambda j: sum_copy(j).start())
    gin[lane] = gsum[lane]
    weigh(TICKS - 2)
    weigh(TICKS - 1)
    for d in range(PLACES):
        for side in range(2):
            start = d * HEAD_SIZE + side * half
            grad[:, :, start : start + HEAD_SIZE] = acc[
                :, d, :, side * HEAD_SIZE : (side + 1) * HEAD_SIZE
            ].astype(B16)
    each(1, lanes, lambda j: sum_copy(j).wait())
    gain_out[...] = jnp.sum(gin[...], axis=0).astype(B16)

    def out_wait(k):
        to = lax.rem(place + k, PLACES)
        out_copy(to).wait_send()
        remote(
            newc.at[TICKS - 1, to], out.at[:, cols(to * wide, wide)],
            co_s.at[to], co_r.at[to], fsdp=at_place(to),
        ).wait_recv()

    each(1, PLACES, out_wait)
    each(1, PLACES, lambda k: cot_copy(k).wait_send())
    each(1, lanes, lambda j: gain_copy(j).wait_send())
    for i in range(2):
        for k in range(4):
            for side in range(2):
                each(1, lanes, lambda j: w_copy(i, k, side, j).wait_send())
    for tick in range(TICKS):
        each(1, PLACES, lambda k: x_copy(tick, k).wait_send())
        each(1, PLACES, lambda k: meta_copy(tick, k).wait_send())
        each(1, lanes, lambda j: q_copy(tick, j).wait_send())
        partner_copy(tick).wait_send()

        def finish(m):
            for copy in near_copies(tick, m):
                copy.wait_send()
            each(1, lanes, lambda j: lane_copy(tick, m, j).wait_send())
            if tick < TICKS - 1:
                pipe_copy(tick, m).wait_send()

            @pl.when(is_mid == 1)
            def _():
                for slot in (1, 2):
                    for copy in pass_copies(tick, m, slot):
                        copy.wait_send()

        each(0, PLACES, finish)

        @pl.when(is_mid == 1)
        def _():
            for k in range(2):
                far_copy(tick, k).wait_send()

        @pl.when(is_mid == 0)
        def _():
            for k in range(2):
                end_copy(tick, k).wait_send()


def relay(n, sections, saved, cot, w, gains, lengths, segments):
    ticks, rows, model = saved.shape
    width, kvw = w.shape[1:]
    lanes = n // PLACES
    wide = model // PLACES
    members = PLACES * rows
    pair = 2 * HEAD_SIZE
    vmem = pl.BlockSpec(memory_space=pltpu.VMEM)
    dma = pltpu.SemaphoreType.DMA
    return pl.pallas_call(
        functools.partial(relay_kernel, n, sections),
        out_shape=(
            jax.ShapeDtypeStruct((rows, model), B16),
            jax.ShapeDtypeStruct(w.shape, B16),
            jax.ShapeDtypeStruct(gains.shape, B16),
        ),
        in_specs=[vmem, vmem, pl.BlockSpec(memory_space=pl.ANY), vmem, vmem, vmem],
        out_specs=(vmem,) * 3,
        scratch_shapes=[
            pltpu.VMEM((ticks, rows, model), B16),
            pltpu.VMEM((ticks, PLACES, rows, wide), B16),
            pltpu.VMEM((ticks, members, wide), B16),
            pltpu.VMEM((lanes, ticks, members, width), B16),
            pltpu.VMEM((ticks, PLACES, rows, wide), B16),
            pltpu.VMEM((PLACES, ticks, 8, HEAD_SIZE), F32),
            pltpu.VMEM((lanes, 2, width), F32),
            pltpu.VMEM((2, lanes * width, kvw), B16),
            pltpu.VMEM((ticks, 3, members, pair), B16),
            pltpu.VMEM((2, members, pair), F32),
            pltpu.VMEM((ticks, 2, members, pair), B16),
            pltpu.VMEM((ticks, 2, members, pair), B16),
            pltpu.VMEM((ticks, members, pair), F32),
            pltpu.VMEM((ticks, PLACES, rows, pair), B16),
            pltpu.VMEM((lanes, ticks, PLACES, PLACES, rows, pair), B16),
            pltpu.VMEM((ticks, PLACES, PLACES, 8, HEAD_SIZE), F32),
            pltpu.VMEM((PLACES, rows, wide), B16),
            pltpu.VMEM((ticks, PLACES, rows, wide), B16),
            pltpu.VMEM((2, PLACES, width, pair), F32),
            pltpu.VMEM((2, 8, wide), F32),
            pltpu.VMEM((lanes, 2, width), F32),
            pltpu.VMEM((lanes, 2, width), F32),
        ]
        + [dma((ticks, PLACES))] * 2
        + [dma((PLACES,))] * 2
        + [dma((ticks, PLACES))] * 2
        + [dma((lanes,))] * 2
        + [dma((2, 4, 2, lanes))] * 2
        + [dma((2,))]
        + [dma((ticks, 2))] * 2
        + [dma((ticks, 3)), dma((ticks, 2))]
        + [dma((ticks, PLACES, 4)), dma((ticks, PLACES, 3))]
        + [dma((ticks, PLACES, 4)), dma((ticks, PLACES, 3))]
        + [dma((ticks, lanes))] * 2
        + [dma((ticks, PLACES, lanes))] * 2
        + [dma((ticks, PLACES))] * 2
        + [dma((PLACES,))] * 2
        + [dma((lanes,))] * 2,
        compiler_params=pltpu.CompilerParams(
            collective_id=0, has_side_effects=True, vmem_limit_bytes=56 * 1024 * 1024
        ),
    )(saved, cot, w, gains, lengths, segments)


def handed_on_kernel(*refs):
    count = len(refs) // 2
    copies = [
        pltpu.make_async_copy(refs[i], refs[count + i], refs[-1].at[i]) for i in range(count)
    ]
    for copy in copies:
        copy.start()
    for copy in copies:
        copy.wait()


def handed_on(*values):
    anywhere = pl.BlockSpec(memory_space=pl.ANY)
    return pl.pallas_call(
        handed_on_kernel,
        out_shape=tuple(jax.ShapeDtypeStruct(v.shape, v.dtype) for v in values),
        in_specs=[pl.BlockSpec(memory_space=pltpu.VMEM)] * len(values),
        out_specs=(anywhere,) * len(values),
        scratch_shapes=[pltpu.SemaphoreType.DMA((len(values),))],
    )(*values)


def body(saved, cot_in, weights, gains, lengths, segments):
    out, grad_kv, grad_gain = relay(
        lax.axis_size("fsdp"), lax.axis_size("pipe"),
        saved[0, 0], cot_in[0, 0], weights[:, 0], gains[:, 0], lengths.T, segments[:, 0],
    )
    out, grad_kv, grad_gain = handed_on(out, grad_kv, grad_gain)
    return out[None, None], grad_kv[:, None], grad_gain[:, None]


def solution(mesh):
    in_specs = (
        P("pipe", "fsdp", None, None, None),
        P("pipe", "fsdp", None, None),
        P(None, "pipe", "fsdp", None),
        P(None, "pipe", "fsdp"),
        P(None, "fsdp"),
        P(None, "fsdp", None),
    )
    out_specs = (
        P("pipe", "fsdp", None, None),
        P(None, "pipe", "fsdp", None),
        P(None, "pipe", "fsdp"),
    )
    return jax.shard_map(body, mesh=mesh, in_specs=in_specs, out_specs=out_specs, check_vma=False)
```

```python
import functools

import jax
import jax.numpy as jnp
from jax import lax
from jax.experimental import pallas as pl
from jax.experimental.pallas import tpu as pltpu
from jax.sharding import PartitionSpec as P

HEAD_SIZE = 128
PLACES = 4
TICKS = 3
EPS = 1e-05
MESH = pl.DeviceIdType.MESH
LIMIT = 56 * 1024 * 1024
F32 = jnp.float32
B16 = jnp.bfloat16
ACROSS = (((1,), (1,)), ((), ()))
DOWN = (((0,), (0,)), ((), ()))
PLAIN = (((1,), (0,)), ((), ()))


def dot(left, right, dims):
    return lax.dot_general(left, right, dims, preferred_element_type=F32)


def remote(src, dst, send, recv, **where):
    return pltpu.make_async_remote_copy(
        src_ref=src,
        dst_ref=dst,
        send_sem=send,
        recv_sem=recv,
        device_id=where,
        device_id_type=MESH,
    )


def each(low, high, step):
    def one(i, _):
        step(i)
        return 0

    lax.fori_loop(low, high, one, 0)


def relay_kernel(
    n, sections,
    saved_in, cot, w, gains_in, lengths_in, segments_in,
    out, grad, gain_out,
    saved, gains, lengths, segments,
    xs, xin, qb, qh, cotb, metab, gb, w2, parts, far, ends, kvin, own, kvb,
    kcb, statb, qcb, newc, acc, gacc, gsum, gin, held,
    x_s, x_r, c_s, c_r, m_s, m_r, g_s, g_r, w_s, w_r, l_s, re_s, re_r, rk_s, rk_r,
    ag_s, ag_r, st_s, st_r, qh_s, qh_r, kl_s, kl_r, pp_s, pp_r, co_s, co_r, gg_s, gg_r,
    h_s, h_r, in_s,
):
    me = lax.axis_index("fsdp")
    section = lax.axis_index("pipe")
    lanes = n // PLACES
    place, lane = lax.div(me, lanes), lax.rem(me, lanes)
    rows, model = cot.shape
    wide = model // PLACES
    width = w.shape[1]
    half = w.shape[2] // 2
    members = PLACES * rows
    partner = place + 1 - 2 * lax.rem(place, 2)
    upper = lax.div(place, 2)
    is_mid = lax.rem(lax.rem(place, 2) + upper, 2)
    far_mid, far_end = 2 - upper, 3 - 3 * upper
    dests = (lax.rem(place + 2, PLACES), PLACES - 1 - place, partner, place)
    below = lax.rem(section + sections - 1, sections)
    above = lax.rem(section + 1, sections)
    across = lax.rem(section + sections // 2, sections)
    loaded = section < sections // 2

    def layer_of(tick):
        item = lax.rem(section + tick, sections)
        return item, lax.rem(item, 2) * sections + item - tick

    def stretch_of(tick):
        return lax.div(jnp.maximum(layer_of(tick)[1], 0), sections)

    first = stretch_of(0)
    second = 1 - first

    def when_active(tick, step):
        if tick:
            pl.when(layer_of(tick)[1] >= 0)(step)
        else:
            step()

    def at_place(other):
        return other * lanes + lane

    def at_lane(j):
        return place * lanes + lax.rem(lane + j, lanes)

    def cols(start, size):
        return pl.ds(pl.multiple_of(start, size), size)

    loads = [
        pltpu.make_async_copy(saved_in.at[0], saved.at[0], in_s.at[0]),
        pltpu.make_async_copy(lengths_in, lengths, in_s.at[3]),
        pltpu.make_async_copy(segments_in, segments, in_s.at[4]),
        pltpu.make_async_copy(gains_in, gains, in_s.at[5]),
        pltpu.make_async_copy(saved_in.at[1], saved.at[1], in_s.at[1]),
        pltpu.make_async_copy(saved_in.at[2], saved.at[2], in_s.at[2]),
    ]
    for load in loads:
        load.start()

    barrier = pltpu.get_barrier_semaphore()

    def greet(**where):
        pl.semaphore_signal(barrier, inc=1, device_id=where, device_id_type=MESH)

    each(1, PLACES, lambda k: greet(fsdp=at_place(lax.rem(place + k, PLACES))))
    each(1, lanes, lambda j: greet(fsdp=at_lane(j)))
    greet(pipe=below)
    greet(pipe=above)
    greet(pipe=across)
    greet(pipe=across, fsdp=at_place(dests[0]))

    def own_w(i, stretch):
        mine = cols(lane * width, width)
        return pltpu.make_async_copy(w.at[stretch], w2.at[stretch, mine], l_s.at[i])

    own_w(0, first).start()
    own_w(1, second).start()

    def normalize(tick):
        x = saved[tick].astype(F32)
        factor = lax.rsqrt(jnp.mean(x * x, axis=-1, keepdims=True) + EPS)
        xs[tick] = (x * factor).astype(B16)
        item, _ = layer_of(tick)
        turned = jnp.transpose(jnp.broadcast_to(factor, (rows, HEAD_SIZE)))[0:1]
        doc = segments[pl.ds(item, 1), :].astype(F32)
        at = lax.broadcasted_iota(jnp.int32, lengths.shape, 1)
        used = jnp.sum(jnp.where(at == item, lengths[...].astype(F32), 0.0), axis=1, keepdims=True)
        metab[place, tick] = jnp.concatenate(
            [
                jnp.concatenate([turned, turned], axis=1),
                jnp.concatenate([doc, doc], axis=1),
                jnp.broadcast_to(used, (1, HEAD_SIZE)),
                jnp.zeros((5, HEAD_SIZE), F32),
            ],
            axis=0,
        )

    for load in loads[:4]:
        load.wait()
    normalize(0)
    gb[lane] = gains[...].astype(F32)
    pl.semaphore_wait(barrier, PLACES - 1 + lanes - 1 + 4)

    def x_copy(tick, k):
        to = lax.rem(place + k, PLACES)
        return remote(
            xs.at[tick, :, cols(to * wide, wide)], xin.at[tick, place],
            x_s.at[tick, k], x_r.at[tick, k], fsdp=at_place(to),
        )

    def relay_copy(tick):
        return remote(
            xs.at[tick, :, cols(dests[0] * wide, wide)], held.at[tick],
            h_s.at[tick], h_r.at[tick], pipe=across,
        )

    def relayed_copy(tick):
        return remote(
            held.at[tick], xin.at[tick, place],
            h_s.at[tick], x_r.at[tick, 2], pipe=across, fsdp=at_place(dests[0]),
        )

    def start_far(tick):
        @pl.when(section >= sections // 2)
        def _():
            relay_copy(tick).wait_recv()
            relayed_copy(tick).start()
            when_active(tick, lambda: x_copy(tick, 2).start())

    def start_next(tick):
        @functools.partial(when_active, tick)
        def _():
            x_copy(tick, 1).start()
            x_copy(tick, 3).start()

    def cot_copy(k):
        to = lax.rem(place + k, PLACES)
        return remote(
            cot.at[:, cols(to * wide, wide)], cotb.at[0, place],
            c_s.at[k], c_r.at[k], fsdp=at_place(to),
        )

    def meta_copy(tick, k):
        to = lax.rem(place + k, PLACES)
        return remote(
            metab.at[place, tick], metab.at[place, tick],
            m_s.at[tick, k], m_r.at[tick, k], fsdp=at_place(to),
        )

    def gain_copy(j):
        return remote(gb.at[lane], gb.at[lane], g_s.at[j], g_r.at[j], fsdp=at_lane(j))

    def w_copy(i, k, side, j):
        stretch = (first, second)[i]
        here = cols(dests[k] * HEAD_SIZE + side * half, HEAD_SIZE)
        return remote(
            w.at[stretch, :, here], w2.at[stretch, cols(lane * width, width), here],
            w_s.at[i, k, side, j], w_r.at[i, k, side, j], fsdp=at_lane(j),
        )

    def send_w(i):
        for k in range(4):
            for side in range(2):
                each(1, lanes, lambda j: w_copy(i, k, side, j).start())

    each(1, lanes, lambda j: gain_copy(j).start())
    each(1, PLACES, lambda k: x_copy(0, k).start())
    send_w(0)
    each(1, PLACES, lambda k: meta_copy(0, k).start())
    each(1, PLACES, lambda k: cot_copy(k).start())
    send_w(1)

    xin[0, place] = xs[0, :, cols(place * wide, wide)]
    own_cot = pltpu.make_async_copy(cot.at[:, cols(place * wide, wide)], cotb.at[0, place], c_s.at[0])
    own_cot.start()
    for tick in (1, 2):
        loads[3 + tick].wait()
        normalize(tick)
        each(1, PLACES, lambda k: meta_copy(tick, k).start())
        xin[tick, place] = xs[tick, :, cols(place * wide, wide)]

        @pl.when(loaded)
        def _():
            relay_copy(tick).start()

    acc[...] = jnp.zeros_like(acc)
    gacc[...] = jnp.zeros_like(gacc)
    each(1, lanes, lambda j: gain_copy(j).wait_recv())

    def gain_of(tick):
        stretch = stretch_of(tick)
        return jnp.concatenate(
            [gb[i, pl.ds(stretch, 1), :] for i in range(lanes)], axis=1
        )

    def q_copy(tick, j):
        to = lax.rem(lane + j, lanes)
        return remote(
            qb.at[tick, :, cols(to * width, width)], qh.at[lane, tick],
            qh_s.at[tick, j], qh_r.at[tick, j], fsdp=at_lane(j),
        )

    def end_copy(tick, k):
        return remote(
            parts.at[tick, k], ends.at[tick, k],
            re_s.at[tick, k], re_r.at[tick, k], fsdp=at_place(partner),
        )

    def partner_copy(tick):
        return remote(
            parts.at[tick, 2], kvin.at[tick, 0],
            rk_s.at[tick, 2], rk_r.at[tick, 0], fsdp=at_place(partner),
        )

    def far_copy(tick, k):
        return remote(
            parts.at[tick, k], kvin.at[tick, 1],
            rk_s.at[tick, k], rk_r.at[tick, 1], fsdp=at_place(dests[k]),
        )

    def take_w(i, k):
        for side in range(2):
            each(1, lanes, lambda j: w_copy(i, k, side, j).wait_recv())

    def forward(tick):
        stretch = stretch_of(tick)
        each(1, PLACES, lambda k: x_copy(tick, k).wait_recv())
        q = (xin[tick].reshape(members, wide).astype(F32) * gain_of(tick)).astype(B16)
        qb[tick] = q
        each(1, lanes, lambda j: q_copy(tick, j).start())
        if tick < 2:
            own_w(tick, (first, second)[tick]).wait()
        for k in range(4):
            if tick < 2:
                take_w(tick, k)
            at = [cols(dests[k] * HEAD_SIZE + side * half, HEAD_SIZE) for side in range(2)]
            right = jnp.concatenate([w2[stretch, :, a] for a in at], axis=1)
            part = dot(qb[tick], right, PLAIN)
            if k < 2:
                far[k] = part

                @pl.when(is_mid == 0)
                def _():
                    parts[tick, k] = far[k].astype(B16)
                    end_copy(tick, k).start()

            elif k == 2:
                parts[tick, 2] = part.astype(B16)
                partner_copy(tick).start()
            else:
                own[tick] = part

    def combine(tick):
        @pl.when(is_mid == 1)
        def _():
            for k in range(2):
                end_copy(tick, 1 - k).wait_recv()
                parts[tick, k] = (far[k] + ends[tick, 1 - k].astype(F32)).astype(B16)
                far_copy(tick, k).start()

    def gather_kv(tick):
        partner_copy(tick).wait_recv()
        far_copy(tick, 0).wait_recv()
        total = own[tick] + kvin[tick, 0].astype(F32) + kvin[tick, 1].astype(F32)
        kvb[tick] = total.astype(B16).reshape(PLACES, rows, 2 * HEAD_SIZE)

    def pipe_copy(tick, m):
        return remote(
            newc.at[tick, m], cotb.at[tick + 1, m],
            pp_s.at[tick, m], pp_r.at[tick, m], pipe=below,
        )

    def near_copies(tick, m, which=(0, 1)):
        chunk, stat = kcb.at[lane, tick, place, m], statb.at[tick, place, m]
        copies = []
        for i in which:
            to, slot = ((partner, 0), (far_mid, 2 - is_mid))[i]
            for ref, send, recv in ((chunk, ag_s, ag_r), (stat, st_s, st_r)):
                copies.append(
                    remote(ref, ref, send.at[tick, m, i], recv.at[tick, m, slot],
                           fsdp=at_place(to))
                )
        return copies

    def pass_copies(tick, m, slot):
        source = (far_mid, far_end)[slot - 1]
        chunk, stat = kcb.at[lane, tick, source, m], statb.at[tick, source, m]
        return [
            remote(chunk, chunk, ag_s.at[tick, m, 1 + slot], ag_r.at[tick, m, slot],
                   fsdp=at_place(partner)),
            remote(stat, stat, st_s.at[tick, m, 1 + slot], st_r.at[tick, m, slot],
                   fsdp=at_place(partner)),
        ]

    def pass_on(tick, m):
        @pl.when(is_mid == 1)
        def _():
            for slot in (1, 2):
                for copy in pass_copies(tick, m, slot):
                    copy.wait_recv()
                    copy.start()

    def heads(value):
        return jnp.concatenate(
            [
                value[:, i * HEAD_SIZE : (i + 1) * HEAD_SIZE]
                for i in range(wide // HEAD_SIZE)
            ],
            axis=0,
        )

    groups = wide // HEAD_SIZE
    scale = HEAD_SIZE ** (-0.5)

    def attend(tick, m):
        if tick:
            pipe_copy(tick - 1, m).wait_recv()
        query = heads(qb[tick, pl.ds(pl.multiple_of(m * rows, rows), rows), :])
        pulled = heads(cotb[tick, m])
        keys = kvb[tick, m, :, :HEAD_SIZE]
        values = kvb[tick, m, :, HEAD_SIZE:]
        meta = metab[m, tick]
        turned = jnp.transpose(meta)

        def tiled(row):
            return jnp.concatenate([meta[row : row + 1]] * (groups * rows // HEAD_SIZE), axis=1)

        shape = (rows, groups * rows)
        spot = lax.broadcasted_iota(jnp.int32, shape, 0)
        seer = lax.rem(lax.broadcasted_iota(jnp.int32, shape, 1), rows)
        key_spot = lax.broadcasted_iota(jnp.int32, (rows, 1), 0).astype(F32)
        doc = jnp.where(key_spot < turned[:rows, 2:3], turned[:rows, 1:2], -1.0)
        seen = ((doc == tiled(1)) & (spot <= seer)) | (spot == seer)
        row_spot = seer[0:1].astype(F32)
        valid = jnp.where(row_spot < tiled(2), 1.0, 0.0)
        raw = dot(keys, query, ACROSS)
        scores = jnp.where(seen, raw * scale, -1e30)
        expo = jnp.exp(scores - jnp.max(scores, axis=0, keepdims=True))
        probs = expo / jnp.sum(expo, axis=0, keepdims=True)
        prob_cot = dot(values, pulled, ACROSS).astype(B16).astype(F32) * valid
        inner = jnp.sum(probs * prob_cot, axis=0, keepdims=True)
        score_cot = jnp.where(seen, probs * (prob_cot - inner), 0.0) * scale
        score_b = score_cot.astype(B16)
        query_cot = dot(score_b, keys, DOWN)
        for i in range(groups):
            qcb[m, :, i * HEAD_SIZE : (i + 1) * HEAD_SIZE] = query_cot[
                i * rows : (i + 1) * rows
            ].astype(B16)
        key_cot = dot(score_b, query, PLAIN).astype(B16)
        value_cot = dot((probs * valid).astype(B16), pulled, PLAIN).astype(B16)
        kcb[lane, tick, place, m, :, :HEAD_SIZE] = key_cot
        kcb[lane, tick, place, m, :, HEAD_SIZE:] = value_cot
        line = jnp.sum(score_cot * raw, axis=0, keepdims=True)
        while line.shape[1] > HEAD_SIZE:
            cut = line.shape[1] // 2
            line = line[:, :cut] + line[:, cut:]
        line = line + pltpu.roll(line, rows, 1)
        both = keys.astype(F32) * key_cot.astype(F32) + values.astype(F32) * value_cot.astype(F32)
        high = both.astype(B16)
        low = (both - high.astype(F32)).astype(B16)
        ones = jnp.ones((8, HEAD_SIZE), B16)
        flat = dot(ones, high, ACROSS) + dot(ones, low, ACROSS)
        statb[tick, place, m] = jnp.concatenate([flat, flat], axis=1) + line
        for copy in near_copies(tick, m):
            copy.start()

    def lane_copy(tick, m, j):
        chunk = kcb.at[lane, tick, :, m]
        return remote(chunk, chunk, kl_s.at[tick, m, j], kl_r.at[tick, m, j], fsdp=at_lane(j))

    def out_copy(m):
        return remote(
            newc.at[TICKS - 1, m], out.at[:, cols(place * wide, wide)],
            co_s.at[m], co_r.at[place], fsdp=at_place(m),
        )

    def settle(tick, m):
        stretch = stretch_of(tick)
        for copy in near_copies(tick, m, (0,)):
            copy.wait_recv()

        @pl.when(is_mid == 0)
        def _():
            for slot in (1, 2):
                for copy in pass_copies(tick, m, slot):
                    copy.wait_recv()

        each(1, lanes, lambda j: lane_copy(tick, m, j).start())
        kc = jnp.concatenate(
            [
                kcb[lane, tick, d, m, :, side * HEAD_SIZE : (side + 1) * HEAD_SIZE]
                for side in range(2)
                for d in range(PLACES)
            ],
            axis=1,
        )
        total = qcb[m].astype(F32) + dot(kc, w2[stretch], ACROSS)
        stat = statb[tick, 0, m]
        for d in range(1, PLACES):
            stat = stat + statb[tick, d, m]
        mean = jnp.transpose(stat)[:rows, 0:1] * (1.0 / model)
        factor = jnp.transpose(metab[m, tick])[:rows, 0:1]
        xhat = xin[tick, m].astype(F32)
        gain = gain_of(tick)
        gacc[stretch] += jnp.sum((xhat * total).reshape(rows // 8, 8, wide), axis=0)
        x_cot = factor * (gain * total - xhat * mean)
        fresh = (cotb[tick, m].astype(F32) + x_cot).astype(B16)
        newc[tick, m] = fresh
        hand_down(tick, m)

    def hand_down(tick, m):
        if tick < TICKS - 1:
            pipe_copy(tick, m).start()
        else:

            @pl.when(m == place)
            def _():
                out[:, cols(place * wide, wide)] = newc[tick, m]

            @pl.when(m != place)
            def _():
                out_copy(m).start()

    def weigh(tick):
        stretch = stretch_of(tick)
        qh[lane, tick] = qb[tick, :, cols(lane * width, width)]
        each(1, lanes, lambda j: q_copy(tick, j).wait_recv())
        each(0, PLACES, lambda m: each(1, lanes, lambda j: lane_copy(tick, m, j).wait_recv()))

        def one(d):
            total = acc[stretch, d]
            for i in range(lanes):
                right = kcb[i, tick, d].reshape(members, 2 * HEAD_SIZE)
                total = total + dot(qh[i, tick], right, DOWN)
            acc[stretch, d] = total

        each(0, PLACES, one)

    forward(0)
    combine(0)
    start_far(1)
    start_next(1)
    each(1, PLACES, lambda k: meta_copy(0, k).wait_recv())
    each(1, PLACES, lambda k: cot_copy(k).wait_recv())
    own_cot.wait()
    for tick in range(TICKS):

        @functools.partial(when_active, tick)
        def _():
            gather_kv(tick)
            each(0, PLACES, lambda m: attend(tick, m))
            pass_on(tick, 0)

        if tick < TICKS - 1:
            when_active(tick + 1, lambda: forward(tick + 1))
        if tick == 0:

            @pl.when(layer_of(1)[1] < 0)
            def _():
                own_w(1, second).wait()
                for k in range(4):
                    take_w(1, k)

        if tick == 0:
            start_far(2)

        def step(i):
            @pl.when(i < PLACES - 1)
            def _():
                pass_on(tick, i + 1)

            settle(tick, i)

        when_active(tick, lambda: each(0, PLACES, step))
        if tick:

            def unchanged(m):
                pipe_copy(tick - 1, m).wait_recv()
                newc[tick, m] = cotb[tick, m]
                hand_down(tick, m)

            pl.when(layer_of(tick)[1] < 0)(lambda: each(0, PLACES, unchanged))
        if tick == 0:
            start_next(2)
        if tick < TICKS - 1:
            when_active(tick + 1, lambda: combine(tick + 1))
            each(1, PLACES, lambda k: meta_copy(tick + 1, k).wait_recv())
            if tick:
                when_active(tick - 1, lambda: weigh(tick - 1))

    gain_sum = jnp.sum(gacc[...], axis=1)
    for i in range(lanes):
        gsum[i] = gain_sum[:, i * width : (i + 1) * width]

    def sum_copy(j):
        to = lax.rem(lane + j, lanes)
        return remote(gsum.at[to], gin.at[lane], gg_s.at[j], gg_r.at[j], fsdp=at_lane(j))

    each(1, lanes, lambda j: sum_copy(j).start())
    gin[lane] = gsum[lane]
    when_active(TICKS - 2, lambda: weigh(TICKS - 2))
    when_active(TICKS - 1, lambda: weigh(TICKS - 1))
    for d in range(PLACES):
        for side in range(2):
            start = d * HEAD_SIZE + side * half
            grad[:, :, start : start + HEAD_SIZE] = acc[
                :, d, :, side * HEAD_SIZE : (side + 1) * HEAD_SIZE
            ].astype(B16)
    each(1, lanes, lambda j: sum_copy(j).wait())
    gain_out[...] = jnp.sum(gin[...], axis=0).astype(B16)

    def out_wait(k):
        to = lax.rem(place + k, PLACES)
        out_copy(to).wait_send()
        remote(
            newc.at[TICKS - 1, to], out.at[:, cols(to * wide, wide)],
            co_s.at[to], co_r.at[to], fsdp=at_place(to),
        ).wait_recv()

    each(1, PLACES, out_wait)
    each(1, PLACES, lambda k: cot_copy(k).wait_send())
    each(1, lanes, lambda j: gain_copy(j).wait_send())
    for i in range(2):
        for k in range(4):
            for side in range(2):
                each(1, lanes, lambda j: w_copy(i, k, side, j).wait_send())
    for tick in range(TICKS):
        each(1, PLACES, lambda k: meta_copy(tick, k).wait_send())
        if tick:
            relay_copy(tick).wait_send()
        if tick < TICKS - 1:
            each(0, PLACES, lambda m: pipe_copy(tick, m).wait_send())

        @functools.partial(when_active, tick)
        def _():
            if tick:
                x_copy(tick, 1).wait_send()
                pl.when(jnp.logical_not(loaded))(lambda: x_copy(tick, 2).wait_send())
                x_copy(tick, 3).wait_send()
            else:
                each(1, PLACES, lambda k: x_copy(tick, k).wait_send())
            each(1, lanes, lambda j: q_copy(tick, j).wait_send())
            partner_copy(tick).wait_send()

            def finish(m):
                for copy in near_copies(tick, m):
                    copy.wait_send()
                each(1, lanes, lambda j: lane_copy(tick, m, j).wait_send())

                @pl.when(is_mid == 1)
                def _():
                    for slot in (1, 2):
                        for copy in pass_copies(tick, m, slot):
                            copy.wait_send()

            each(0, PLACES, finish)

            @pl.when(is_mid == 1)
            def _():
                for k in range(2):
                    far_copy(tick, k).wait_send()

            @pl.when(is_mid == 0)
            def _():
                for k in range(2):
                    end_copy(tick, k).wait_send()


def relay(n, sections, saved, cot, w, gains, lengths, segments):
    ticks, rows, model = saved.shape
    width, kvw = w.shape[1:]
    lanes = n // PLACES
    wide = model // PLACES
    members = PLACES * rows
    pair = 2 * HEAD_SIZE
    vmem = pl.BlockSpec(memory_space=pltpu.VMEM)
    dma = pltpu.SemaphoreType.DMA
    return pl.pallas_call(
        functools.partial(relay_kernel, n, sections),
        out_shape=(
            jax.ShapeDtypeStruct((rows, model), B16),
            jax.ShapeDtypeStruct(w.shape, B16),
            jax.ShapeDtypeStruct(gains.shape, B16),
        ),
        in_specs=[pl.BlockSpec(memory_space=pltpu.HBM)] * 6,
        out_specs=(vmem,) * 3,
        scratch_shapes=[
            pltpu.VMEM(saved.shape, B16),
            pltpu.VMEM(gains.shape, B16),
            pltpu.VMEM(lengths.shape, jnp.int32),
            pltpu.VMEM(segments.shape, jnp.int32),
            pltpu.VMEM((ticks, rows, model), B16),
            pltpu.VMEM((ticks, PLACES, rows, wide), B16),
            pltpu.VMEM((ticks, members, wide), B16),
            pltpu.VMEM((lanes, ticks, members, width), B16),
            pltpu.VMEM((ticks, PLACES, rows, wide), B16),
            pltpu.VMEM((PLACES, ticks, 8, HEAD_SIZE), F32),
            pltpu.VMEM((lanes, 2, width), F32),
            pltpu.VMEM((2, lanes * width, kvw), B16),
            pltpu.VMEM((ticks, 3, members, pair), B16),
            pltpu.VMEM((2, members, pair), F32),
            pltpu.VMEM((ticks, 2, members, pair), B16),
            pltpu.VMEM((ticks, 2, members, pair), B16),
            pltpu.VMEM((ticks, members, pair), F32),
            pltpu.VMEM((ticks, PLACES, rows, pair), B16),
            pltpu.VMEM((lanes, ticks, PLACES, PLACES, rows, pair), B16),
            pltpu.VMEM((ticks, PLACES, PLACES, 8, HEAD_SIZE), F32),
            pltpu.VMEM((PLACES, rows, wide), B16),
            pltpu.VMEM((ticks, PLACES, rows, wide), B16),
            pltpu.VMEM((2, PLACES, width, pair), F32),
            pltpu.VMEM((2, 8, wide), F32),
            pltpu.VMEM((lanes, 2, width), F32),
            pltpu.VMEM((lanes, 2, width), F32),
            pltpu.VMEM((ticks, rows, wide), B16),
        ]
        + [dma((ticks, PLACES))] * 2
        + [dma((PLACES,))] * 2
        + [dma((ticks, PLACES))] * 2
        + [dma((lanes,))] * 2
        + [dma((2, 4, 2, lanes))] * 2
        + [dma((2,))]
        + [dma((ticks, 2))] * 2
        + [dma((ticks, 3)), dma((ticks, 2))]
        + [dma((ticks, PLACES, 4)), dma((ticks, PLACES, 3))]
        + [dma((ticks, PLACES, 4)), dma((ticks, PLACES, 3))]
        + [dma((ticks, lanes))] * 2
        + [dma((ticks, PLACES, lanes))] * 2
        + [dma((ticks, PLACES))] * 2
        + [dma((PLACES,))] * 2
        + [dma((lanes,))] * 2
        + [dma((ticks,))] * 2
        + [dma((6,))],
        compiler_params=pltpu.CompilerParams(
            collective_id=0, has_side_effects=True, vmem_limit_bytes=LIMIT
        ),
    )(saved, cot, w, gains, lengths, segments)


def handed_on_kernel(out, grad, gain, to_out, to_grad, to_gain, out_v, grad_v, gain_v, sems):
    half = grad.shape[1] // 2
    routes = [(out, out_v, to_out), (gain, gain_v, to_gain)]
    for stretch in range(2):
        for start in (0, half):
            routes.append([ref.at[stretch, start : start + half] for ref in (grad, grad_v, to_grad)])
    ins = [pltpu.make_async_copy(a, b, sems.at[0, i]) for i, (a, b, _) in enumerate(routes)]
    outs = [pltpu.make_async_copy(b, c, sems.at[1, i]) for i, (_, b, c) in enumerate(routes)]
    for copy in ins:
        copy.start()
    for i, copy in enumerate(outs):
        ins[i].wait()
        copy.start()
    for copy in outs:
        copy.wait()


def handed_on(*values):
    anywhere = pl.BlockSpec(memory_space=pl.ANY)
    return pl.pallas_call(
        handed_on_kernel,
        out_shape=tuple(jax.ShapeDtypeStruct(v.shape, v.dtype) for v in values),
        in_specs=[anywhere] * len(values),
        out_specs=(anywhere,) * len(values),
        scratch_shapes=[pltpu.VMEM(v.shape, v.dtype) for v in values]
        + [pltpu.SemaphoreType.DMA((2, 6))],
        compiler_params=pltpu.CompilerParams(vmem_limit_bytes=LIMIT),
    )(*values)


def body(saved, cot_in, weights, gains, lengths, segments):
    out, grad_kv, grad_gain = relay(
        lax.axis_size("fsdp"), lax.axis_size("pipe"),
        saved[0, 0], cot_in[0, 0], weights[:, 0], gains[:, 0], lengths.T, segments[:, 0],
    )
    out, grad_kv, grad_gain = handed_on(out, grad_kv, grad_gain)
    return out[None, None], grad_kv[:, None], grad_gain[:, None]


def solution(mesh):
    in_specs = (
        P("pipe", "fsdp", None, None, None),
        P("pipe", "fsdp", None, None),
        P(None, "pipe", "fsdp", None),
        P(None, "pipe", "fsdp"),
        P(None, "fsdp"),
        P(None, "fsdp", None),
    )
    out_specs = (
        P("pipe", "fsdp", None, None),
        P(None, "pipe", "fsdp", None),
        P(None, "pipe", "fsdp"),
    )
    return jax.shard_map(body, mesh=mesh, in_specs=in_specs, out_specs=out_specs, check_vma=False)
```

```python
import functools

import jax
import jax.numpy as jnp
from jax import lax
from jax.experimental import pallas as pl
from jax.experimental.pallas import tpu as pltpu
from jax.sharding import PartitionSpec as P

HEAD_SIZE = 128
PLACES = 4
TICKS = 3
EPS = 1e-05
MESH = pl.DeviceIdType.MESH
LIMIT = 56 * 1024 * 1024
F32 = jnp.float32
B16 = jnp.bfloat16
ACROSS = (((1,), (1,)), ((), ()))
DOWN = (((0,), (0,)), ((), ()))
PLAIN = (((1,), (0,)), ((), ()))


def dot(left, right, dims):
    return lax.dot_general(left, right, dims, preferred_element_type=F32)


def remote(src, dst, send, recv, **where):
    return pltpu.make_async_remote_copy(
        src_ref=src,
        dst_ref=dst,
        send_sem=send,
        recv_sem=recv,
        device_id=where,
        device_id_type=MESH,
    )


def each(low, high, step):
    def one(i, _):
        step(i)
        return 0

    lax.fori_loop(low, high, one, 0)


def relay_kernel(
    n, sections,
    saved_in, cot, w, gains_in, lengths_in, segments_in,
    out, grad, gain_out,
    saved, gains, lengths, segments,
    xs, xin, qb, qh, cotb, metab, gb, w2, parts, far, ends, kvin, own, kvb,
    kcb, statb, qcb, newc, acc, gacc, gsum, gin, held, held_w,
    x_s, x_r, c_s, c_r, m_s, m_r, g_s, g_r, w_s, w_r, l_s, re_s, re_r, rk_s, rk_r,
    ag_s, ag_r, st_s, st_r, qh_s, qh_r, kl_s, kl_r, pp_s, pp_r, co_s, co_r, gg_s, gg_r,
    h_s, h_r, hw_s, hw_r, in_s,
):
    me = lax.axis_index("fsdp")
    section = lax.axis_index("pipe")
    lanes = n // PLACES
    place, lane = lax.div(me, lanes), lax.rem(me, lanes)
    rows, model = cot.shape
    wide = model // PLACES
    width = w.shape[1]
    half = w.shape[2] // 2
    members = PLACES * rows
    partner = place + 1 - 2 * lax.rem(place, 2)
    upper = lax.div(place, 2)
    is_mid = lax.rem(lax.rem(place, 2) + upper, 2)
    far_mid, far_end = 2 - upper, 3 - 3 * upper
    dests = (lax.rem(place + 2, PLACES), PLACES - 1 - place, partner, place)
    below = lax.rem(section + sections - 1, sections)
    above = lax.rem(section + 1, sections)
    across = lax.rem(section + sections // 2, sections)
    loaded = section < sections // 2

    def layer_of(tick):
        item = lax.rem(section + tick, sections)
        return item, lax.rem(item, 2) * sections + item - tick

    def stretch_of(tick):
        return lax.div(jnp.maximum(layer_of(tick)[1], 0), sections)

    first = stretch_of(0)
    second = 1 - first

    def when_active(tick, step):
        if tick:
            pl.when(layer_of(tick)[1] >= 0)(step)
        else:
            step()

    def at_place(other):
        return other * lanes + lane

    def at_lane(j):
        return place * lanes + lax.rem(lane + j, lanes)

    def cols(start, size):
        return pl.ds(pl.multiple_of(start, size), size)

    loads = [
        pltpu.make_async_copy(saved_in.at[0], saved.at[0], in_s.at[0]),
        pltpu.make_async_copy(lengths_in, lengths, in_s.at[3]),
        pltpu.make_async_copy(segments_in, segments, in_s.at[4]),
        pltpu.make_async_copy(gains_in, gains, in_s.at[5]),
        pltpu.make_async_copy(saved_in.at[1], saved.at[1], in_s.at[1]),
        pltpu.make_async_copy(saved_in.at[2], saved.at[2], in_s.at[2]),
    ]
    for load in loads:
        load.start()

    barrier = pltpu.get_barrier_semaphore()

    def greet(**where):
        pl.semaphore_signal(barrier, inc=1, device_id=where, device_id_type=MESH)

    each(1, PLACES, lambda k: greet(fsdp=at_place(lax.rem(place + k, PLACES))))
    each(1, lanes, lambda j: greet(fsdp=at_lane(j)))
    greet(pipe=below)
    greet(pipe=above)
    greet(pipe=across)
    greet(pipe=across, fsdp=at_place(dests[0]))
    each(1, lanes, lambda j: greet(pipe=across, fsdp=at_lane(j)))

    def own_w(i, stretch):
        mine = cols(lane * width, width)
        return pltpu.make_async_copy(w.at[stretch], w2.at[stretch, mine], l_s.at[i])

    own_w(0, first).start()
    own_w(1, second).start()

    def normalize(tick):
        x = saved[tick].astype(F32)
        factor = lax.rsqrt(jnp.mean(x * x, axis=-1, keepdims=True) + EPS)
        xs[tick] = (x * factor).astype(B16)
        item, _ = layer_of(tick)
        turned = jnp.transpose(jnp.broadcast_to(factor, (rows, HEAD_SIZE)))[0:1]
        doc = segments[pl.ds(item, 1), :].astype(F32)
        at = lax.broadcasted_iota(jnp.int32, lengths.shape, 1)
        used = jnp.sum(jnp.where(at == item, lengths[...].astype(F32), 0.0), axis=1, keepdims=True)
        metab[place, tick] = jnp.concatenate(
            [
                jnp.concatenate([turned, turned], axis=1),
                jnp.concatenate([doc, doc], axis=1),
                jnp.broadcast_to(used, (1, HEAD_SIZE)),
                jnp.zeros((5, HEAD_SIZE), F32),
            ],
            axis=0,
        )

    for load in loads[:4]:
        load.wait()
    normalize(0)
    gb[lane] = gains[...].astype(F32)
    pl.semaphore_wait(barrier, PLACES - 1 + 2 * (lanes - 1) + 4)

    def x_copy(tick, k):
        to = lax.rem(place + k, PLACES)
        return remote(
            xs.at[tick, :, cols(to * wide, wide)], xin.at[tick, place],
            x_s.at[tick, k], x_r.at[tick, k], fsdp=at_place(to),
        )

    def relay_copy(tick):
        return remote(
            xs.at[tick, :, cols(dests[0] * wide, wide)], held.at[tick],
            h_s.at[tick], h_r.at[tick], pipe=across,
        )

    def relayed_copy(tick):
        return remote(
            held.at[tick], xin.at[tick, place],
            h_s.at[tick], x_r.at[tick, 2], pipe=across, fsdp=at_place(dests[0]),
        )

    def start_far(tick):
        @pl.when(section >= sections // 2)
        def _():
            if tick == 1:
                each(1, lanes, pass_second)
            relay_copy(tick).wait_recv()
            relayed_copy(tick).start()
            when_active(tick, lambda: x_copy(tick, 2).start())

    def start_next(tick):
        @functools.partial(when_active, tick)
        def _():
            x_copy(tick, 1).start()
            x_copy(tick, 3).start()

    def cot_copy(k):
        to = lax.rem(place + k, PLACES)
        return remote(
            cot.at[:, cols(to * wide, wide)], cotb.at[0, place],
            c_s.at[k], c_r.at[k], fsdp=at_place(to),
        )

    def meta_copy(tick, k):
        to = lax.rem(place + k, PLACES)
        return remote(
            metab.at[place, tick], metab.at[place, tick],
            m_s.at[tick, k], m_r.at[tick, k], fsdp=at_place(to),
        )

    def gain_copy(j):
        return remote(gb.at[lane], gb.at[lane], g_s.at[j], g_r.at[j], fsdp=at_lane(j))

    def w_copy(i, k, side, j):
        stretch = (first, second)[i]
        here = cols(dests[k] * HEAD_SIZE + side * half, HEAD_SIZE)
        return remote(
            w.at[stretch, :, here], w2.at[stretch, cols(lane * width, width), here],
            w_s.at[i, k, side, j], w_r.at[i, k, side, j], fsdp=at_lane(j),
        )

    def send_w(i, ks=range(4)):
        for k in ks:
            for side in range(2):
                each(1, lanes, lambda j: w_copy(i, k, side, j).start())

    def wrelay_copy(side, j):
        here = cols(place * HEAD_SIZE + side * half, HEAD_SIZE)
        return remote(
            w.at[second, :, here], held_w.at[j, side],
            hw_s.at[side, j], hw_r.at[side, j], pipe=across, fsdp=at_lane(j),
        )

    def wrelayed_copy(side, j):
        here = cols(place * HEAD_SIZE + side * half, HEAD_SIZE)
        there = cols(lax.rem(lane - j + lanes, lanes) * width, width)
        return remote(
            held_w.at[j, side], w2.at[1 - lax.rem(across, 2), there, here],
            hw_s.at[side, j], w_r.at[1, 3, side, j], pipe=across,
        )

    def send_second():
        @pl.when(loaded)
        def _():
            for side in range(2):
                each(1, lanes, lambda j: wrelay_copy(side, j).start())

        send_w(1, range(3))

        @pl.when(jnp.logical_not(loaded))
        def _():
            send_w(1, (3,))

    def pass_second(j):
        for side in range(2):
            wrelay_copy(side, j).wait_recv()
            wrelayed_copy(side, j).start()

    each(1, lanes, lambda j: gain_copy(j).start())
    each(1, PLACES, lambda k: x_copy(0, k).start())
    send_w(0)
    each(1, PLACES, lambda k: meta_copy(0, k).start())
    each(1, PLACES, lambda k: cot_copy(k).start())
    send_second()

    xin[0, place] = xs[0, :, cols(place * wide, wide)]
    own_cot = pltpu.make_async_copy(cot.at[:, cols(place * wide, wide)], cotb.at[0, place], c_s.at[0])
    own_cot.start()
    for tick in (1, 2):
        loads[3 + tick].wait()
        normalize(tick)
        each(1, PLACES, lambda k: meta_copy(tick, k).start())
        xin[tick, place] = xs[tick, :, cols(place * wide, wide)]

        @pl.when(loaded)
        def _():
            relay_copy(tick).start()

    acc[...] = jnp.zeros_like(acc)
    gacc[...] = jnp.zeros_like(gacc)
    each(1, lanes, lambda j: gain_copy(j).wait_recv())

    def gain_of(tick):
        stretch = stretch_of(tick)
        return jnp.concatenate(
            [gb[i, pl.ds(stretch, 1), :] for i in range(lanes)], axis=1
        )

    def q_copy(tick, j):
        to = lax.rem(lane + j, lanes)
        return remote(
            qb.at[tick, :, cols(to * width, width)], qh.at[lane, tick],
            qh_s.at[tick, j], qh_r.at[tick, j], fsdp=at_lane(j),
        )

    def end_copy(tick, k):
        return remote(
            parts.at[tick, k], ends.at[tick, k],
            re_s.at[tick, k], re_r.at[tick, k], fsdp=at_place(partner),
        )

    def partner_copy(tick):
        return remote(
            parts.at[tick, 2], kvin.at[tick, 0],
            rk_s.at[tick, 2], rk_r.at[tick, 0], fsdp=at_place(partner),
        )

    def far_copy(tick, k):
        return remote(
            parts.at[tick, k], kvin.at[tick, 1],
            rk_s.at[tick, k], rk_r.at[tick, 1], fsdp=at_place(dests[k]),
        )

    def take_w(i, k):
        for side in range(2):
            each(1, lanes, lambda j: w_copy(i, k, side, j).wait_recv())

    def forward(tick):
        stretch = stretch_of(tick)
        each(1, PLACES, lambda k: x_copy(tick, k).wait_recv())
        q = (xin[tick].reshape(members, wide).astype(F32) * gain_of(tick)).astype(B16)
        qb[tick] = q
        each(1, lanes, lambda j: q_copy(tick, j).start())
        if tick < 2:
            own_w(tick, (first, second)[tick]).wait()
        for k in range(4):
            if tick < 2:
                take_w(tick, k)
            at = [cols(dests[k] * HEAD_SIZE + side * half, HEAD_SIZE) for side in range(2)]
            right = jnp.concatenate([w2[stretch, :, a] for a in at], axis=1)
            part = dot(qb[tick], right, PLAIN)
            if k < 2:
                far[k] = part

                @pl.when(is_mid == 0)
                def _():
                    parts[tick, k] = far[k].astype(B16)
                    end_copy(tick, k).start()

            elif k == 2:
                parts[tick, 2] = part.astype(B16)
                partner_copy(tick).start()
            else:
                own[tick] = part

    def combine(tick):
        @pl.when(is_mid == 1)
        def _():
            for k in range(2):
                end_copy(tick, 1 - k).wait_recv()
                parts[tick, k] = (far[k] + ends[tick, 1 - k].astype(F32)).astype(B16)
                far_copy(tick, k).start()

    def gather_kv(tick):
        partner_copy(tick).wait_recv()
        far_copy(tick, 0).wait_recv()
        total = own[tick] + kvin[tick, 0].astype(F32) + kvin[tick, 1].astype(F32)
        kvb[tick] = total.astype(B16).reshape(PLACES, rows, 2 * HEAD_SIZE)

    def pipe_copy(tick, m):
        return remote(
            newc.at[tick, m], cotb.at[tick + 1, m],
            pp_s.at[tick, m], pp_r.at[tick, m], pipe=below,
        )

    def near_copies(tick, m, which=(0, 1)):
        chunk, stat = kcb.at[lane, tick, place, m], statb.at[tick, place, m]
        copies = []
        for i in which:
            to, slot = ((partner, 0), (far_mid, 2 - is_mid))[i]
            for ref, send, recv in ((chunk, ag_s, ag_r), (stat, st_s, st_r)):
                copies.append(
                    remote(ref, ref, send.at[tick, m, i], recv.at[tick, m, slot],
                           fsdp=at_place(to))
                )
        return copies

    def pass_copies(tick, m, slot):
        source = (far_mid, far_end)[slot - 1]
        chunk, stat = kcb.at[lane, tick, source, m], statb.at[tick, source, m]
        return [
            remote(chunk, chunk, ag_s.at[tick, m, 1 + slot], ag_r.at[tick, m, slot],
                   fsdp=at_place(partner)),
            remote(stat, stat, st_s.at[tick, m, 1 + slot], st_r.at[tick, m, slot],
                   fsdp=at_place(partner)),
        ]

    def pass_on(tick, m):
        @pl.when(is_mid == 1)
        def _():
            for slot in (1, 2):
                for copy in pass_copies(tick, m, slot):
                    copy.wait_recv()
                    copy.start()

    def heads(value):
        return jnp.concatenate(
            [
                value[:, i * HEAD_SIZE : (i + 1) * HEAD_SIZE]
                for i in range(wide // HEAD_SIZE)
            ],
            axis=0,
        )

    groups = wide // HEAD_SIZE
    scale = HEAD_SIZE ** (-0.5)

    def attend(tick, m):
        if tick:
            pipe_copy(tick - 1, m).wait_recv()
        query = heads(qb[tick, pl.ds(pl.multiple_of(m * rows, rows), rows), :])
        pulled = heads(cotb[tick, m])
        keys = kvb[tick, m, :, :HEAD_SIZE]
        values = kvb[tick, m, :, HEAD_SIZE:]
        meta = metab[m, tick]
        turned = jnp.transpose(meta)

        def tiled(row):
            return jnp.concatenate([meta[row : row + 1]] * (groups * rows // HEAD_SIZE), axis=1)

        shape = (rows, groups * rows)
        spot = lax.broadcasted_iota(jnp.int32, shape, 0)
        seer = lax.rem(lax.broadcasted_iota(jnp.int32, shape, 1), rows)
        key_spot = lax.broadcasted_iota(jnp.int32, (rows, 1), 0).astype(F32)
        doc = jnp.where(key_spot < turned[:rows, 2:3], turned[:rows, 1:2], -1.0)
        seen = ((doc == tiled(1)) & (spot <= seer)) | (spot == seer)
        row_spot = seer[0:1].astype(F32)
        valid = jnp.where(row_spot < tiled(2), 1.0, 0.0)
        raw = dot(keys, query, ACROSS)
        scores = jnp.where(seen, raw * scale, -1e30)
        expo = jnp.exp(scores - jnp.max(scores, axis=0, keepdims=True))
        probs = expo / jnp.sum(expo, axis=0, keepdims=True)
        prob_cot = dot(values, pulled, ACROSS).astype(B16).astype(F32) * valid
        inner = jnp.sum(probs * prob_cot, axis=0, keepdims=True)
        score_cot = jnp.where(seen, probs * (prob_cot - inner), 0.0) * scale
        score_b = score_cot.astype(B16)
        query_cot = dot(score_b, keys, DOWN)
        for i in range(groups):
            qcb[m, :, i * HEAD_SIZE : (i + 1) * HEAD_SIZE] = query_cot[
                i * rows : (i + 1) * rows
            ].astype(B16)
        key_cot = dot(score_b, query, PLAIN).astype(B16)
        value_cot = dot((probs * valid).astype(B16), pulled, PLAIN).astype(B16)
        kcb[lane, tick, place, m, :, :HEAD_SIZE] = key_cot
        kcb[lane, tick, place, m, :, HEAD_SIZE:] = value_cot
        line = jnp.sum(score_cot * raw, axis=0, keepdims=True)
        while line.shape[1] > HEAD_SIZE:
            cut = line.shape[1] // 2
            line = line[:, :cut] + line[:, cut:]
        line = line + pltpu.roll(line, rows, 1)
        both = keys.astype(F32) * key_cot.astype(F32) + values.astype(F32) * value_cot.astype(F32)
        high = both.astype(B16)
        low = (both - high.astype(F32)).astype(B16)
        ones = jnp.ones((8, HEAD_SIZE), B16)
        flat = dot(ones, high, ACROSS) + dot(ones, low, ACROSS)
        statb[tick, place, m] = jnp.concatenate([flat, flat], axis=1) + line
        for copy in near_copies(tick, m):
            copy.start()

    def lane_copy(tick, m, j):
        chunk = kcb.at[lane, tick, :, m]
        return remote(chunk, chunk, kl_s.at[tick, m, j], kl_r.at[tick, m, j], fsdp=at_lane(j))

    def out_copy(m):
        return remote(
            newc.at[TICKS - 1, m], out.at[:, cols(place * wide, wide)],
            co_s.at[m], co_r.at[place], fsdp=at_place(m),
        )

    def settle(tick, m):
        stretch = stretch_of(tick)
        for copy in near_copies(tick, m, (0,)):
            copy.wait_recv()

        @pl.when(is_mid == 0)
        def _():
            for slot in (1, 2):
                for copy in pass_copies(tick, m, slot):
                    copy.wait_recv()

        each(1, lanes, lambda j: lane_copy(tick, m, j).start())
        kc = jnp.concatenate(
            [
                kcb[lane, tick, d, m, :, side * HEAD_SIZE : (side + 1) * HEAD_SIZE]
                for side in range(2)
                for d in range(PLACES)
            ],
            axis=1,
        )
        total = qcb[m].astype(F32) + dot(kc, w2[stretch], ACROSS)
        stat = statb[tick, 0, m]
        for d in range(1, PLACES):
            stat = stat + statb[tick, d, m]
        mean = jnp.transpose(stat)[:rows, 0:1] * (1.0 / model)
        factor = jnp.transpose(metab[m, tick])[:rows, 0:1]
        xhat = xin[tick, m].astype(F32)
        gain = gain_of(tick)
        gacc[stretch] += jnp.sum((xhat * total).reshape(rows // 8, 8, wide), axis=0)
        x_cot = factor * (gain * total - xhat * mean)
        fresh = (cotb[tick, m].astype(F32) + x_cot).astype(B16)
        newc[tick, m] = fresh
        hand_down(tick, m)

    def relay_out(m):
        return remote(
            newc.at[TICKS - 1, m], held.at[0], h_s.at[0], h_r.at[0], pipe=across
        )

    def relayed_out():
        return remote(
            held.at[0], out.at[:, cols(place * wide, wide)],
            h_s.at[0], co_r.at[place], pipe=across, fsdp=at_place(dests[0]),
        )

    def hand_down(tick, m):
        if tick < TICKS - 1:
            pipe_copy(tick, m).start()
        else:

            @pl.when(m == place)
            def _():
                out[:, cols(place * wide, wide)] = newc[tick, m]

            relayed = loaded & (m == dests[0])

            @pl.when(relayed)
            def _():
                relay_out(m).start()

            @pl.when((m != place) & jnp.logical_not(relayed))
            def _():
                out_copy(m).start()

    def weigh(tick):
        stretch = stretch_of(tick)
        qh[lane, tick] = qb[tick, :, cols(lane * width, width)]
        each(1, lanes, lambda j: q_copy(tick, j).wait_recv())
        each(0, PLACES, lambda m: each(1, lanes, lambda j: lane_copy(tick, m, j).wait_recv()))

        def one(d):
            total = acc[stretch, d]
            for i in range(lanes):
                right = kcb[i, tick, d].reshape(members, 2 * HEAD_SIZE)
                total = total + dot(qh[i, tick], right, DOWN)
            acc[stretch, d] = total

        each(0, PLACES, one)

    forward(0)
    start_next(1)
    combine(0)
    start_far(1)
    each(1, PLACES, lambda k: meta_copy(0, k).wait_recv())
    each(1, PLACES, lambda k: cot_copy(k).wait_recv())
    own_cot.wait()
    for tick in range(TICKS):

        @functools.partial(when_active, tick)
        def _():
            gather_kv(tick)
            each(0, PLACES, lambda m: attend(tick, m))
            pass_on(tick, 0)

        if tick < TICKS - 1:
            when_active(tick + 1, lambda: forward(tick + 1))
        if tick == 0:

            @pl.when(layer_of(1)[1] < 0)
            def _():
                own_w(1, second).wait()
                for k in range(4):
                    take_w(1, k)

        if tick == 0:
            start_far(2)

        def step(i):
            @pl.when(i < PLACES - 1)
            def _():
                pass_on(tick, i + 1)

            settle(tick, i)

        when_active(tick, lambda: each(0, PLACES, step))
        if tick:

            def unchanged(m):
                pipe_copy(tick - 1, m).wait_recv()
                newc[tick, m] = cotb[tick, m]
                hand_down(tick, m)

            pl.when(layer_of(tick)[1] < 0)(lambda: each(0, PLACES, unchanged))
        if tick == 0:
            start_next(2)
        if tick < TICKS - 1:
            when_active(tick + 1, lambda: combine(tick + 1))
            each(1, PLACES, lambda k: meta_copy(tick + 1, k).wait_recv())
            if tick:
                when_active(tick - 1, lambda: weigh(tick - 1))

    gain_sum = jnp.sum(gacc[...], axis=1)
    for i in range(lanes):
        gsum[i] = gain_sum[:, i * width : (i + 1) * width]

    def sum_copy(j):
        to = lax.rem(lane + j, lanes)
        return remote(gsum.at[to], gin.at[lane], gg_s.at[j], gg_r.at[j], fsdp=at_lane(j))

    each(1, lanes, lambda j: sum_copy(j).start())
    gin[lane] = gsum[lane]
    when_active(TICKS - 2, lambda: weigh(TICKS - 2))
    when_active(TICKS - 1, lambda: weigh(TICKS - 1))

    @pl.when(jnp.logical_not(loaded))
    def _():
        relay_out(dests[0]).wait_recv()
        relayed_out().start()

    for d in range(PLACES):
        for side in range(2):
            start = d * HEAD_SIZE + side * half
            grad[:, :, start : start + HEAD_SIZE] = acc[
                :, d, :, side * HEAD_SIZE : (side + 1) * HEAD_SIZE
            ].astype(B16)
    each(1, lanes, lambda j: sum_copy(j).wait())
    gain_out[...] = jnp.sum(gin[...], axis=0).astype(B16)

    def out_wait(k):
        to = lax.rem(place + k, PLACES)
        if k == 2:
            relay_out(to).wait_send()
            pl.when(jnp.logical_not(loaded))(lambda: out_copy(to).wait_send())
        else:
            out_copy(to).wait_send()
        remote(
            newc.at[TICKS - 1, to], out.at[:, cols(to * wide, wide)],
            co_s.at[to], co_r.at[to], fsdp=at_place(to),
        ).wait_recv()

    for k in range(1, PLACES):
        out_wait(k)
    each(1, PLACES, lambda k: cot_copy(k).wait_send())
    each(1, lanes, lambda j: gain_copy(j).wait_send())
    for side in range(2):
        for i in range(2):
            for k in range(4 - i):
                each(1, lanes, lambda j: w_copy(i, k, side, j).wait_send())
        each(1, lanes, lambda j: wrelay_copy(side, j).wait_send())

        @pl.when(jnp.logical_not(loaded))
        def _():
            each(1, lanes, lambda j: w_copy(1, 3, side, j).wait_send())
    for tick in range(TICKS):
        each(1, PLACES, lambda k: meta_copy(tick, k).wait_send())
        if tick:
            relay_copy(tick).wait_send()
        if tick < TICKS - 1:
            each(0, PLACES, lambda m: pipe_copy(tick, m).wait_send())

        @functools.partial(when_active, tick)
        def _():
            if tick:
                x_copy(tick, 1).wait_send()
                pl.when(jnp.logical_not(loaded))(lambda: x_copy(tick, 2).wait_send())
                x_copy(tick, 3).wait_send()
            else:
                each(1, PLACES, lambda k: x_copy(tick, k).wait_send())
            each(1, lanes, lambda j: q_copy(tick, j).wait_send())
            partner_copy(tick).wait_send()

            def finish(m):
                for copy in near_copies(tick, m):
                    copy.wait_send()
                each(1, lanes, lambda j: lane_copy(tick, m, j).wait_send())

                @pl.when(is_mid == 1)
                def _():
                    for slot in (1, 2):
                        for copy in pass_copies(tick, m, slot):
                            copy.wait_send()

            each(0, PLACES, finish)

            @pl.when(is_mid == 1)
            def _():
                for k in range(2):
                    far_copy(tick, k).wait_send()

            @pl.when(is_mid == 0)
            def _():
                for k in range(2):
                    end_copy(tick, k).wait_send()


def relay(n, sections, saved, cot, w, gains, lengths, segments):
    ticks, rows, model = saved.shape
    width, kvw = w.shape[1:]
    lanes = n // PLACES
    wide = model // PLACES
    members = PLACES * rows
    pair = 2 * HEAD_SIZE
    vmem = pl.BlockSpec(memory_space=pltpu.VMEM)
    dma = pltpu.SemaphoreType.DMA
    return pl.pallas_call(
        functools.partial(relay_kernel, n, sections),
        out_shape=(
            jax.ShapeDtypeStruct((rows, model), B16),
            jax.ShapeDtypeStruct(w.shape, B16),
            jax.ShapeDtypeStruct(gains.shape, B16),
        ),
        in_specs=[pl.BlockSpec(memory_space=pltpu.HBM)] * 6,
        out_specs=(vmem,) * 3,
        scratch_shapes=[
            pltpu.VMEM(saved.shape, B16),
            pltpu.VMEM(gains.shape, B16),
            pltpu.VMEM(lengths.shape, jnp.int32),
            pltpu.VMEM(segments.shape, jnp.int32),
            pltpu.VMEM((ticks, rows, model), B16),
            pltpu.VMEM((ticks, PLACES, rows, wide), B16),
            pltpu.VMEM((ticks, members, wide), B16),
            pltpu.VMEM((lanes, ticks, members, width), B16),
            pltpu.VMEM((ticks, PLACES, rows, wide), B16),
            pltpu.VMEM((PLACES, ticks, 8, HEAD_SIZE), F32),
            pltpu.VMEM((lanes, 2, width), F32),
            pltpu.VMEM((2, lanes * width, kvw), B16),
            pltpu.VMEM((ticks, 3, members, pair), B16),
            pltpu.VMEM((2, members, pair), F32),
            pltpu.VMEM((ticks, 2, members, pair), B16),
            pltpu.VMEM((ticks, 2, members, pair), B16),
            pltpu.VMEM((ticks, members, pair), F32),
            pltpu.VMEM((ticks, PLACES, rows, pair), B16),
            pltpu.VMEM((lanes, ticks, PLACES, PLACES, rows, pair), B16),
            pltpu.VMEM((ticks, PLACES, PLACES, 8, HEAD_SIZE), F32),
            pltpu.VMEM((PLACES, rows, wide), B16),
            pltpu.VMEM((ticks, PLACES, rows, wide), B16),
            pltpu.VMEM((2, PLACES, width, pair), F32),
            pltpu.VMEM((2, 8, wide), F32),
            pltpu.VMEM((lanes, 2, width), F32),
            pltpu.VMEM((lanes, 2, width), F32),
            pltpu.VMEM((ticks, rows, wide), B16),
            pltpu.VMEM((lanes, 2, width, HEAD_SIZE), B16),
        ]
        + [dma((ticks, PLACES))] * 2
        + [dma((PLACES,))] * 2
        + [dma((ticks, PLACES))] * 2
        + [dma((lanes,))] * 2
        + [dma((2, 4, 2, lanes))] * 2
        + [dma((2,))]
        + [dma((ticks, 2))] * 2
        + [dma((ticks, 3)), dma((ticks, 2))]
        + [dma((ticks, PLACES, 4)), dma((ticks, PLACES, 3))]
        + [dma((ticks, PLACES, 4)), dma((ticks, PLACES, 3))]
        + [dma((ticks, lanes))] * 2
        + [dma((ticks, PLACES, lanes))] * 2
        + [dma((ticks, PLACES))] * 2
        + [dma((PLACES,))] * 2
        + [dma((lanes,))] * 2
        + [dma((ticks,))] * 2
        + [dma((2, lanes))] * 2
        + [dma((6,))],
        compiler_params=pltpu.CompilerParams(
            collective_id=0, has_side_effects=True, vmem_limit_bytes=LIMIT
        ),
    )(saved, cot, w, gains, lengths, segments)


def handed_on_kernel(out, grad, gain, to_out, to_grad, to_gain, out_v, grad_v, gain_v, sems):
    half = grad.shape[1] // 2
    routes = [(out, out_v, to_out), (gain, gain_v, to_gain)]
    for stretch in range(2):
        for start in (0, half):
            routes.append([ref.at[stretch, start : start + half] for ref in (grad, grad_v, to_grad)])
    ins = [pltpu.make_async_copy(a, b, sems.at[0, i]) for i, (a, b, _) in enumerate(routes)]
    outs = [pltpu.make_async_copy(b, c, sems.at[1, i]) for i, (_, b, c) in enumerate(routes)]
    for copy in ins:
        copy.start()
    for i, copy in enumerate(outs):
        ins[i].wait()
        copy.start()
    for copy in outs:
        copy.wait()


def handed_on(*values):
    anywhere = pl.BlockSpec(memory_space=pl.ANY)
    return pl.pallas_call(
        handed_on_kernel,
        out_shape=tuple(jax.ShapeDtypeStruct(v.shape, v.dtype) for v in values),
        in_specs=[anywhere] * len(values),
        out_specs=(anywhere,) * len(values),
        scratch_shapes=[pltpu.VMEM(v.shape, v.dtype) for v in values]
        + [pltpu.SemaphoreType.DMA((2, 6))],
        compiler_params=pltpu.CompilerParams(vmem_limit_bytes=LIMIT),
    )(*values)


def body(saved, cot_in, weights, gains, lengths, segments):
    out, grad_kv, grad_gain = relay(
        lax.axis_size("fsdp"), lax.axis_size("pipe"),
        saved[0, 0], cot_in[0, 0], weights[:, 0], gains[:, 0], lengths.T, segments[:, 0],
    )
    out, grad_kv, grad_gain = handed_on(out, grad_kv, grad_gain)
    return out[None, None], grad_kv[:, None], grad_gain[:, None]


def solution(mesh):
    in_specs = (
        P("pipe", "fsdp", None, None, None),
        P("pipe", "fsdp", None, None),
        P(None, "pipe", "fsdp", None),
        P(None, "pipe", "fsdp"),
        P(None, "fsdp"),
        P(None, "fsdp", None),
    )
    out_specs = (
        P("pipe", "fsdp", None, None),
        P(None, "pipe", "fsdp", None),
        P(None, "pipe", "fsdp"),
    )
    return jax.shard_map(body, mesh=mesh, in_specs=in_specs, out_specs=out_specs, check_vma=False)
```

```python
import functools

import jax
import jax.numpy as jnp
from jax import lax
from jax.experimental import pallas as pl
from jax.experimental.pallas import tpu as pltpu
from jax.sharding import PartitionSpec as P

HEAD_SIZE = 128
PLACES = 4
TICKS = 3
EPS = 1e-05
MESH = pl.DeviceIdType.MESH
LIMIT = 56 * 1024 * 1024
F32 = jnp.float32
B16 = jnp.bfloat16
ACROSS = (((1,), (1,)), ((), ()))
DOWN = (((0,), (0,)), ((), ()))
PLAIN = (((1,), (0,)), ((), ()))


def dot(left, right, dims):
    return lax.dot_general(left, right, dims, preferred_element_type=F32)


def remote(src, dst, send, recv, **where):
    return pltpu.make_async_remote_copy(
        src_ref=src,
        dst_ref=dst,
        send_sem=send,
        recv_sem=recv,
        device_id=where,
        device_id_type=MESH,
    )


def each(low, high, step):
    def one(i, _):
        step(i)
        return 0

    lax.fori_loop(low, high, one, 0)


def relay_kernel(
    n, sections,
    saved_in, cot, w, gains_in, lengths_in, segments_in,
    out, grad, gain_out,
    saved, gains, lengths, segments,
    xs, xin, qb, qh, cotb, metab, gb, w2, parts, far, ends, kvin, own, kvb,
    kcb, statb, qcb, newc, acc, gacc, gsum, gin, held,
    x_s, x_r, c_s, c_r, m_s, m_r, g_s, g_r, w_s, w_r, l_s, re_s, re_r, rk_s, rk_r,
    ag_s, ag_r, st_s, st_r, qh_s, qh_r, kl_s, kl_r, pp_s, pp_r, co_s, co_r, gg_s, gg_r,
    h_s, h_r, in_s,
):
    me = lax.axis_index("fsdp")
    section = lax.axis_index("pipe")
    lanes = n // PLACES
    place, lane = lax.div(me, lanes), lax.rem(me, lanes)
    rows, model = cot.shape
    wide = model // PLACES
    width = w.shape[1]
    half = w.shape[2] // 2
    members = PLACES * rows
    partner = place + 1 - 2 * lax.rem(place, 2)
    upper = lax.div(place, 2)
    is_mid = lax.rem(lax.rem(place, 2) + upper, 2)
    far_mid, far_end = 2 - upper, 3 - 3 * upper
    dests = (lax.rem(place + 2, PLACES), PLACES - 1 - place, partner, place)
    below = lax.rem(section + sections - 1, sections)
    above = lax.rem(section + 1, sections)
    across = lax.rem(section + sections // 2, sections)
    loaded = section < sections // 2

    def layer_of(tick):
        item = lax.rem(section + tick, sections)
        return item, lax.rem(item, 2) * sections + item - tick

    def stretch_of(tick):
        return lax.div(jnp.maximum(layer_of(tick)[1], 0), sections)

    first = stretch_of(0)
    second = 1 - first

    def when_active(tick, step):
        if tick:
            pl.when(layer_of(tick)[1] >= 0)(step)
        else:
            step()

    def at_place(other):
        return other * lanes + lane

    def at_lane(j):
        return place * lanes + lax.rem(lane + j, lanes)

    def cols(start, size):
        return pl.ds(pl.multiple_of(start, size), size)

    loads = [
        pltpu.make_async_copy(saved_in.at[0], saved.at[0], in_s.at[0]),
        pltpu.make_async_copy(lengths_in, lengths, in_s.at[3]),
        pltpu.make_async_copy(segments_in, segments, in_s.at[4]),
        pltpu.make_async_copy(gains_in, gains, in_s.at[5]),
        pltpu.make_async_copy(saved_in.at[1], saved.at[1], in_s.at[1]),
        pltpu.make_async_copy(saved_in.at[2], saved.at[2], in_s.at[2]),
    ]
    for load in loads:
        load.start()

    barrier = pltpu.get_barrier_semaphore()

    def greet(**where):
        pl.semaphore_signal(barrier, inc=1, device_id=where, device_id_type=MESH)

    each(1, PLACES, lambda k: greet(fsdp=at_place(lax.rem(place + k, PLACES))))
    each(1, lanes, lambda j: greet(fsdp=at_lane(j)))
    greet(pipe=below)
    greet(pipe=above)
    greet(pipe=across)
    greet(pipe=across, fsdp=at_place(dests[0]))

    def own_w(i, stretch):
        mine = cols(lane * width, width)
        return pltpu.make_async_copy(w.at[stretch], w2.at[stretch, mine], l_s.at[i])

    own_w(0, first).start()
    own_w(1, second).start()

    def normalize(tick):
        x = saved[tick].astype(F32)
        factor = lax.rsqrt(jnp.mean(x * x, axis=-1, keepdims=True) + EPS)
        xs[tick] = (x * factor).astype(B16)
        item, _ = layer_of(tick)
        turned = jnp.transpose(jnp.broadcast_to(factor, (rows, HEAD_SIZE)))[0:1]
        doc = segments[pl.ds(item, 1), :].astype(F32)
        at = lax.broadcasted_iota(jnp.int32, lengths.shape, 1)
        used = jnp.sum(jnp.where(at == item, lengths[...].astype(F32), 0.0), axis=1, keepdims=True)
        metab[place, tick] = jnp.concatenate(
            [
                jnp.concatenate([turned, turned], axis=1),
                jnp.concatenate([doc, doc], axis=1),
                jnp.broadcast_to(used, (1, HEAD_SIZE)),
                jnp.zeros((5, HEAD_SIZE), F32),
            ],
            axis=0,
        )

    for load in loads[:4]:
        load.wait()
    normalize(0)
    gb[lane] = gains[...].astype(F32)
    pl.semaphore_wait(barrier, PLACES - 1 + lanes - 1 + 4)

    def x_copy(tick, k):
        to = lax.rem(place + k, PLACES)
        return remote(
            xs.at[tick, :, cols(to * wide, wide)], xin.at[tick, place],
            x_s.at[tick, k], x_r.at[tick, k], fsdp=at_place(to),
        )

    def relay_copy(tick):
        return remote(
            xs.at[tick, :, cols(dests[0] * wide, wide)], held.at[tick],
            h_s.at[tick], h_r.at[tick], pipe=across,
        )

    def relayed_copy(tick):
        return remote(
            held.at[tick], xin.at[tick, place],
            h_s.at[tick], x_r.at[tick, 2], pipe=across, fsdp=at_place(dests[0]),
        )

    def start_far(tick):
        @pl.when(section >= sections // 2)
        def _():
            relay_copy(tick).wait_recv()
            relayed_copy(tick).start()
            when_active(tick, lambda: x_copy(tick, 2).start())

    def start_next(tick):
        @functools.partial(when_active, tick)
        def _():
            x_copy(tick, 1).start()
            x_copy(tick, 3).start()

    def cot_copy(k):
        to = lax.rem(place + k, PLACES)
        return remote(
            cot.at[:, cols(to * wide, wide)], cotb.at[0, place],
            c_s.at[k], c_r.at[k], fsdp=at_place(to),
        )

    def meta_copy(tick, k):
        to = lax.rem(place + k, PLACES)
        return remote(
            metab.at[place, tick], metab.at[place, tick],
            m_s.at[tick, k], m_r.at[tick, k], fsdp=at_place(to),
        )

    def gain_copy(j):
        return remote(gb.at[lane], gb.at[lane], g_s.at[j], g_r.at[j], fsdp=at_lane(j))

    def w_copy(i, k, side, j):
        stretch = (first, second)[i]
        here = cols(dests[k] * HEAD_SIZE + side * half, HEAD_SIZE)
        return remote(
            w.at[stretch, :, here], w2.at[stretch, cols(lane * width, width), here],
            w_s.at[i, k, side, j], w_r.at[i, k, side, j], fsdp=at_lane(j),
        )

    def send_w(i):
        for k in range(4):
            for side in range(2):
                each(1, lanes, lambda j: w_copy(i, k, side, j).start())

    each(1, lanes, lambda j: gain_copy(j).start())
    each(1, PLACES, lambda k: x_copy(0, k).start())
    send_w(0)
    each(1, PLACES, lambda k: meta_copy(0, k).start())
    each(1, PLACES, lambda k: cot_copy(k).start())
    send_w(1)

    xin[0, place] = xs[0, :, cols(place * wide, wide)]
    own_cot = pltpu.make_async_copy(cot.at[:, cols(place * wide, wide)], cotb.at[0, place], c_s.at[0])
    own_cot.start()
    for tick in (1, 2):
        loads[3 + tick].wait()
        normalize(tick)
        each(1, PLACES, lambda k: meta_copy(tick, k).start())
        xin[tick, place] = xs[tick, :, cols(place * wide, wide)]

        @pl.when(loaded)
        def _():
            relay_copy(tick).start()

    acc[...] = jnp.zeros_like(acc)
    gacc[...] = jnp.zeros_like(gacc)
    each(1, lanes, lambda j: gain_copy(j).wait_recv())

    def gain_of(tick):
        stretch = stretch_of(tick)
        return jnp.concatenate(
            [gb[i, pl.ds(stretch, 1), :] for i in range(lanes)], axis=1
        )

    def q_copy(tick, j):
        to = lax.rem(lane + j, lanes)
        return remote(
            qb.at[tick, :, cols(to * width, width)], qh.at[lane, tick],
            qh_s.at[tick, j], qh_r.at[tick, j], fsdp=at_lane(j),
        )

    def end_copy(tick, k):
        return remote(
            parts.at[tick, k], ends.at[tick, k],
            re_s.at[tick, k], re_r.at[tick, k], fsdp=at_place(partner),
        )

    def partner_copy(tick):
        return remote(
            parts.at[tick, 2], kvin.at[tick, 0],
            rk_s.at[tick, 2], rk_r.at[tick, 0], fsdp=at_place(partner),
        )

    def far_copy(tick, k):
        return remote(
            parts.at[tick, k], kvin.at[tick, 1],
            rk_s.at[tick, k], rk_r.at[tick, 1], fsdp=at_place(dests[k]),
        )

    def take_w(i, k):
        for side in range(2):
            each(1, lanes, lambda j: w_copy(i, k, side, j).wait_recv())

    def forward(tick):
        stretch = stretch_of(tick)
        each(1, PLACES, lambda k: x_copy(tick, k).wait_recv())
        q = (xin[tick].reshape(members, wide).astype(F32) * gain_of(tick)).astype(B16)
        qb[tick] = q
        each(1, lanes, lambda j: q_copy(tick, j).start())
        if tick < 2:
            own_w(tick, (first, second)[tick]).wait()
        for k in range(4):
            if tick < 2:
                take_w(tick, k)
            at = [cols(dests[k] * HEAD_SIZE + side * half, HEAD_SIZE) for side in range(2)]
            right = jnp.concatenate([w2[stretch, :, a] for a in at], axis=1)
            part = dot(qb[tick], right, PLAIN)
            if k < 2:
                far[k] = part

                @pl.when(is_mid == 0)
                def _():
                    parts[tick, k] = far[k].astype(B16)
                    end_copy(tick, k).start()

            elif k == 2:
                parts[tick, 2] = part.astype(B16)
                partner_copy(tick).start()
            else:
                own[tick] = part

    def combine(tick):
        @pl.when(is_mid == 1)
        def _():
            for k in range(2):
                end_copy(tick, 1 - k).wait_recv()
                parts[tick, k] = (far[k] + ends[tick, 1 - k].astype(F32)).astype(B16)
                far_copy(tick, k).start()

    def gather_kv(tick):
        partner_copy(tick).wait_recv()
        far_copy(tick, 0).wait_recv()
        total = own[tick] + kvin[tick, 0].astype(F32) + kvin[tick, 1].astype(F32)
        kvb[tick] = total.astype(B16).reshape(PLACES, rows, 2 * HEAD_SIZE)

    def pipe_copy(tick, m):
        return remote(
            newc.at[tick, m], cotb.at[tick + 1, m],
            pp_s.at[tick, m], pp_r.at[tick, m], pipe=below,
        )

    def near_copies(tick, m, which=(0, 1)):
        chunk, stat = kcb.at[lane, tick, place, m], statb.at[tick, place, m]
        copies = []
        for i in which:
            to, slot = ((partner, 0), (far_mid, 2 - is_mid))[i]
            for ref, send, recv in ((chunk, ag_s, ag_r), (stat, st_s, st_r)):
                copies.append(
                    remote(ref, ref, send.at[tick, m, i], recv.at[tick, m, slot],
                           fsdp=at_place(to))
                )
        return copies

    def pass_copies(tick, m, slot):
        source = (far_mid, far_end)[slot - 1]
        chunk, stat = kcb.at[lane, tick, source, m], statb.at[tick, source, m]
        return [
            remote(chunk, chunk, ag_s.at[tick, m, 1 + slot], ag_r.at[tick, m, slot],
                   fsdp=at_place(partner)),
            remote(stat, stat, st_s.at[tick, m, 1 + slot], st_r.at[tick, m, slot],
                   fsdp=at_place(partner)),
        ]

    def pass_on(tick, m):
        @pl.when(is_mid == 1)
        def _():
            for slot in (1, 2):
                for copy in pass_copies(tick, m, slot):
                    copy.wait_recv()
                    copy.start()

    def heads(value):
        return jnp.concatenate(
            [
                value[:, i * HEAD_SIZE : (i + 1) * HEAD_SIZE]
                for i in range(wide // HEAD_SIZE)
            ],
            axis=0,
        )

    groups = wide // HEAD_SIZE
    scale = HEAD_SIZE ** (-0.5)

    def attend(tick, m):
        if tick:
            pipe_copy(tick - 1, m).wait_recv()
        query = heads(qb[tick, pl.ds(pl.multiple_of(m * rows, rows), rows), :])
        pulled = heads(cotb[tick, m])
        keys = kvb[tick, m, :, :HEAD_SIZE]
        values = kvb[tick, m, :, HEAD_SIZE:]
        meta = metab[m, tick]
        turned = jnp.transpose(meta)

        def tiled(row):
            return jnp.concatenate([meta[row : row + 1]] * (groups * rows // HEAD_SIZE), axis=1)

        shape = (rows, groups * rows)
        spot = lax.broadcasted_iota(jnp.int32, shape, 0)
        seer = lax.rem(lax.broadcasted_iota(jnp.int32, shape, 1), rows)
        key_spot = lax.broadcasted_iota(jnp.int32, (rows, 1), 0).astype(F32)
        doc = jnp.where(key_spot < turned[:rows, 2:3], turned[:rows, 1:2], -1.0)
        seen = ((doc == tiled(1)) & (spot <= seer)) | (spot == seer)
        row_spot = seer[0:1].astype(F32)
        valid = jnp.where(row_spot < tiled(2), 1.0, 0.0)
        raw = dot(keys, query, ACROSS)
        scores = jnp.where(seen, raw * scale, -1e30)
        expo = jnp.exp(scores - jnp.max(scores, axis=0, keepdims=True))
        probs = expo / jnp.sum(expo, axis=0, keepdims=True)
        prob_cot = dot(values, pulled, ACROSS).astype(B16).astype(F32) * valid
        inner = jnp.sum(probs * prob_cot, axis=0, keepdims=True)
        score_cot = jnp.where(seen, probs * (prob_cot - inner), 0.0) * scale
        score_b = score_cot.astype(B16)
        query_cot = dot(score_b, keys, DOWN)
        for i in range(groups):
            qcb[m, :, i * HEAD_SIZE : (i + 1) * HEAD_SIZE] = query_cot[
                i * rows : (i + 1) * rows
            ].astype(B16)
        key_cot = dot(score_b, query, PLAIN).astype(B16)
        value_cot = dot((probs * valid).astype(B16), pulled, PLAIN).astype(B16)
        kcb[lane, tick, place, m, :, :HEAD_SIZE] = key_cot
        kcb[lane, tick, place, m, :, HEAD_SIZE:] = value_cot
        line = jnp.sum(score_cot * raw, axis=0, keepdims=True)
        while line.shape[1] > HEAD_SIZE:
            cut = line.shape[1] // 2
            line = line[:, :cut] + line[:, cut:]
        line = line + pltpu.roll(line, rows, 1)
        both = keys.astype(F32) * key_cot.astype(F32) + values.astype(F32) * value_cot.astype(F32)
        high = both.astype(B16)
        low = (both - high.astype(F32)).astype(B16)
        ones = jnp.ones((8, HEAD_SIZE), B16)
        flat = dot(ones, high, ACROSS) + dot(ones, low, ACROSS)
        statb[tick, place, m] = jnp.concatenate([flat, flat], axis=1) + line
        for copy in near_copies(tick, m):
            copy.start()

    def lane_copy(tick, m, j):
        chunk = kcb.at[lane, tick, :, m]
        return remote(chunk, chunk, kl_s.at[tick, m, j], kl_r.at[tick, m, j], fsdp=at_lane(j))

    def out_copy(m):
        return remote(
            newc.at[TICKS - 1, m], out.at[:, cols(place * wide, wide)],
            co_s.at[m], co_r.at[place], fsdp=at_place(m),
        )

    def settle(tick, m):
        stretch = stretch_of(tick)
        for copy in near_copies(tick, m, (0,)):
            copy.wait_recv()

        @pl.when(is_mid == 0)
        def _():
            for slot in (1, 2):
                for copy in pass_copies(tick, m, slot):
                    copy.wait_recv()

        each(1, lanes, lambda j: lane_copy(tick, m, j).start())
        kc = jnp.concatenate(
            [
                kcb[lane, tick, d, m, :, side * HEAD_SIZE : (side + 1) * HEAD_SIZE]
                for side in range(2)
                for d in range(PLACES)
            ],
            axis=1,
        )
        total = qcb[m].astype(F32) + dot(kc, w2[stretch], ACROSS)
        stat = statb[tick, 0, m]
        for d in range(1, PLACES):
            stat = stat + statb[tick, d, m]
        mean = jnp.transpose(stat)[:rows, 0:1] * (1.0 / model)
        factor = jnp.transpose(metab[m, tick])[:rows, 0:1]
        xhat = xin[tick, m].astype(F32)
        gain = gain_of(tick)
        gacc[stretch] += jnp.sum((xhat * total).reshape(rows // 8, 8, wide), axis=0)
        x_cot = factor * (gain * total - xhat * mean)
        fresh = (cotb[tick, m].astype(F32) + x_cot).astype(B16)
        newc[tick, m] = fresh
        hand_down(tick, m)

    def relay_out(m):
        return remote(
            newc.at[TICKS - 1, m], held.at[0], h_s.at[0], h_r.at[0], pipe=across
        )

    def relayed_out():
        return remote(
            held.at[0], out.at[:, cols(place * wide, wide)],
            h_s.at[0], co_r.at[place], pipe=across, fsdp=at_place(dests[0]),
        )

    def hand_down(tick, m):
        if tick < TICKS - 1:
            pipe_copy(tick, m).start()
        else:

            @pl.when(m == place)
            def _():
                out[:, cols(place * wide, wide)] = newc[tick, m]

            relayed = loaded & (m == dests[0])

            @pl.when(relayed)
            def _():
                relay_out(m).start()

            @pl.when((m != place) & jnp.logical_not(relayed))
            def _():
                out_copy(m).start()

    def weigh(tick):
        stretch = stretch_of(tick)
        qh[lane, tick] = qb[tick, :, cols(lane * width, width)]
        each(1, lanes, lambda j: q_copy(tick, j).wait_recv())
        each(0, PLACES, lambda m: each(1, lanes, lambda j: lane_copy(tick, m, j).wait_recv()))

        def one(d):
            total = acc[stretch, d]
            for i in range(lanes):
                right = kcb[i, tick, d].reshape(members, 2 * HEAD_SIZE)
                total = total + dot(qh[i, tick], right, DOWN)
            acc[stretch, d] = total

        each(0, PLACES, one)

    forward(0)
    start_next(1)
    combine(0)
    start_far(1)
    each(1, PLACES, lambda k: meta_copy(0, k).wait_recv())
    each(1, PLACES, lambda k: cot_copy(k).wait_recv())
    own_cot.wait()
    for tick in range(TICKS):

        @functools.partial(when_active, tick)
        def _():
            gather_kv(tick)
            each(0, PLACES, lambda m: attend(tick, m))
            pass_on(tick, 0)

        if tick == TICKS - 1:
            weigh(0)
        if tick < TICKS - 1:
            when_active(tick + 1, lambda: forward(tick + 1))
        if tick == 0:

            @pl.when(layer_of(1)[1] < 0)
            def _():
                own_w(1, second).wait()
                for k in range(4):
                    take_w(1, k)

        if tick == 0:
            start_far(2)

        def step(i):
            @pl.when(i < PLACES - 1)
            def _():
                pass_on(tick, i + 1)

            settle(tick, i)

        when_active(tick, lambda: each(0, PLACES, step))
        if tick:

            def unchanged(m):
                pipe_copy(tick - 1, m).wait_recv()
                newc[tick, m] = cotb[tick, m]
                hand_down(tick, m)

            pl.when(layer_of(tick)[1] < 0)(lambda: each(0, PLACES, unchanged))
        if tick == 0:
            start_next(2)
        if tick < TICKS - 1:
            when_active(tick + 1, lambda: combine(tick + 1))
            each(1, PLACES, lambda k: meta_copy(tick + 1, k).wait_recv())

    gain_sum = jnp.sum(gacc[...], axis=1)
    for i in range(lanes):
        gsum[i] = gain_sum[:, i * width : (i + 1) * width]

    def sum_copy(j):
        to = lax.rem(lane + j, lanes)
        return remote(gsum.at[to], gin.at[lane], gg_s.at[j], gg_r.at[j], fsdp=at_lane(j))

    each(1, lanes, lambda j: sum_copy(j).start())
    gin[lane] = gsum[lane]
    when_active(TICKS - 2, lambda: weigh(TICKS - 2))
    when_active(TICKS - 1, lambda: weigh(TICKS - 1))

    @pl.when(jnp.logical_not(loaded))
    def _():
        relay_out(dests[0]).wait_recv()
        relayed_out().start()

    for d in range(PLACES):
        for side in range(2):
            start = d * HEAD_SIZE + side * half
            grad[:, :, start : start + HEAD_SIZE] = acc[
                :, d, :, side * HEAD_SIZE : (side + 1) * HEAD_SIZE
            ].astype(B16)
    each(1, lanes, lambda j: sum_copy(j).wait())
    gain_out[...] = jnp.sum(gin[...], axis=0).astype(B16)

    def out_wait(k):
        to = lax.rem(place + k, PLACES)
        if k == 2:
            relay_out(to).wait_send()
            pl.when(jnp.logical_not(loaded))(lambda: out_copy(to).wait_send())
        else:
            out_copy(to).wait_send()
        remote(
            newc.at[TICKS - 1, to], out.at[:, cols(to * wide, wide)],
            co_s.at[to], co_r.at[to], fsdp=at_place(to),
        ).wait_recv()

    for k in range(1, PLACES):
        out_wait(k)
    each(1, PLACES, lambda k: cot_copy(k).wait_send())
    each(1, lanes, lambda j: gain_copy(j).wait_send())
    for side in range(2):
        for i in range(2):
            for k in range(4):
                each(1, lanes, lambda j: w_copy(i, k, side, j).wait_send())
    for tick in range(TICKS):
        each(1, PLACES, lambda k: meta_copy(tick, k).wait_send())
        if tick:
            relay_copy(tick).wait_send()
        if tick < TICKS - 1:
            each(0, PLACES, lambda m: pipe_copy(tick, m).wait_send())

        @functools.partial(when_active, tick)
        def _():
            if tick:
                x_copy(tick, 1).wait_send()
                pl.when(jnp.logical_not(loaded))(lambda: x_copy(tick, 2).wait_send())
                x_copy(tick, 3).wait_send()
            else:
                each(1, PLACES, lambda k: x_copy(tick, k).wait_send())
            each(1, lanes, lambda j: q_copy(tick, j).wait_send())
            partner_copy(tick).wait_send()

            def finish(m):
                for copy in near_copies(tick, m):
                    copy.wait_send()
                each(1, lanes, lambda j: lane_copy(tick, m, j).wait_send())

                @pl.when(is_mid == 1)
                def _():
                    for slot in (1, 2):
                        for copy in pass_copies(tick, m, slot):
                            copy.wait_send()

            each(0, PLACES, finish)

            @pl.when(is_mid == 1)
            def _():
                for k in range(2):
                    far_copy(tick, k).wait_send()

            @pl.when(is_mid == 0)
            def _():
                for k in range(2):
                    end_copy(tick, k).wait_send()


def relay(n, sections, saved, cot, w, gains, lengths, segments):
    ticks, rows, model = saved.shape
    width, kvw = w.shape[1:]
    lanes = n // PLACES
    wide = model // PLACES
    members = PLACES * rows
    pair = 2 * HEAD_SIZE
    vmem = pl.BlockSpec(memory_space=pltpu.VMEM)
    dma = pltpu.SemaphoreType.DMA
    return pl.pallas_call(
        functools.partial(relay_kernel, n, sections),
        out_shape=(
            jax.ShapeDtypeStruct((rows, model), B16),
            jax.ShapeDtypeStruct(w.shape, B16),
            jax.ShapeDtypeStruct(gains.shape, B16),
        ),
        in_specs=[pl.BlockSpec(memory_space=pltpu.HBM)] * 6,
        out_specs=(vmem,) * 3,
        scratch_shapes=[
            pltpu.VMEM(saved.shape, B16),
            pltpu.VMEM(gains.shape, B16),
            pltpu.VMEM(lengths.shape, jnp.int32),
            pltpu.VMEM(segments.shape, jnp.int32),
            pltpu.VMEM((ticks, rows, model), B16),
            pltpu.VMEM((ticks, PLACES, rows, wide), B16),
            pltpu.VMEM((ticks, members, wide), B16),
            pltpu.VMEM((lanes, ticks, members, width), B16),
            pltpu.VMEM((ticks, PLACES, rows, wide), B16),
            pltpu.VMEM((PLACES, ticks, 8, HEAD_SIZE), F32),
            pltpu.VMEM((lanes, 2, width), F32),
            pltpu.VMEM((2, lanes * width, kvw), B16),
            pltpu.VMEM((ticks, 3, members, pair), B16),
            pltpu.VMEM((2, members, pair), F32),
            pltpu.VMEM((ticks, 2, members, pair), B16),
            pltpu.VMEM((ticks, 2, members, pair), B16),
            pltpu.VMEM((ticks, members, pair), F32),
            pltpu.VMEM((ticks, PLACES, rows, pair), B16),
            pltpu.VMEM((lanes, ticks, PLACES, PLACES, rows, pair), B16),
            pltpu.VMEM((ticks, PLACES, PLACES, 8, HEAD_SIZE), F32),
            pltpu.VMEM((PLACES, rows, wide), B16),
            pltpu.VMEM((ticks, PLACES, rows, wide), B16),
            pltpu.VMEM((2, PLACES, width, pair), F32),
            pltpu.VMEM((2, 8, wide), F32),
            pltpu.VMEM((lanes, 2, width), F32),
            pltpu.VMEM((lanes, 2, width), F32),
            pltpu.VMEM((ticks, rows, wide), B16),
        ]
        + [dma((ticks, PLACES))] * 2
        + [dma((PLACES,))] * 2
        + [dma((ticks, PLACES))] * 2
        + [dma((lanes,))] * 2
        + [dma((2, 4, 2, lanes))] * 2
        + [dma((2,))]
        + [dma((ticks, 2))] * 2
        + [dma((ticks, 3)), dma((ticks, 2))]
        + [dma((ticks, PLACES, 4)), dma((ticks, PLACES, 3))]
        + [dma((ticks, PLACES, 4)), dma((ticks, PLACES, 3))]
        + [dma((ticks, lanes))] * 2
        + [dma((ticks, PLACES, lanes))] * 2
        + [dma((ticks, PLACES))] * 2
        + [dma((PLACES,))] * 2
        + [dma((lanes,))] * 2
        + [dma((ticks,))] * 2
        + [dma((6,))],
        compiler_params=pltpu.CompilerParams(
            collective_id=0, has_side_effects=True, vmem_limit_bytes=LIMIT
        ),
    )(saved, cot, w, gains, lengths, segments)


def handed_on_kernel(out, grad, gain, to_out, to_grad, to_gain, out_v, grad_v, gain_v, sems):
    half = grad.shape[1] // 2
    routes = [(out, out_v, to_out), (gain, gain_v, to_gain)]
    for stretch in range(2):
        for start in (0, half):
            routes.append([ref.at[stretch, start : start + half] for ref in (grad, grad_v, to_grad)])
    ins = [pltpu.make_async_copy(a, b, sems.at[0, i]) for i, (a, b, _) in enumerate(routes)]
    outs = [pltpu.make_async_copy(b, c, sems.at[1, i]) for i, (_, b, c) in enumerate(routes)]
    for copy in ins:
        copy.start()
    for i, copy in enumerate(outs):
        ins[i].wait()
        copy.start()
    for copy in outs:
        copy.wait()


def handed_on(*values):
    anywhere = pl.BlockSpec(memory_space=pl.ANY)
    return pl.pallas_call(
        handed_on_kernel,
        out_shape=tuple(jax.ShapeDtypeStruct(v.shape, v.dtype) for v in values),
        in_specs=[anywhere] * len(values),
        out_specs=(anywhere,) * len(values),
        scratch_shapes=[pltpu.VMEM(v.shape, v.dtype) for v in values]
        + [pltpu.SemaphoreType.DMA((2, 6))],
        compiler_params=pltpu.CompilerParams(vmem_limit_bytes=LIMIT),
    )(*values)


def body(saved, cot_in, weights, gains, lengths, segments):
    out, grad_kv, grad_gain = relay(
        lax.axis_size("fsdp"), lax.axis_size("pipe"),
        saved[0, 0], cot_in[0, 0], weights[:, 0], gains[:, 0], lengths.T, segments[:, 0],
    )
    out, grad_kv, grad_gain = handed_on(out, grad_kv, grad_gain)
    return out[None, None], grad_kv[:, None], grad_gain[:, None]


def solution(mesh):
    in_specs = (
        P("pipe", "fsdp", None, None, None),
        P("pipe", "fsdp", None, None),
        P(None, "pipe", "fsdp", None),
        P(None, "pipe", "fsdp"),
        P(None, "fsdp"),
        P(None, "fsdp", None),
    )
    out_specs = (
        P("pipe", "fsdp", None, None),
        P(None, "pipe", "fsdp", None),
        P(None, "pipe", "fsdp"),
    )
    return jax.shard_map(body, mesh=mesh, in_specs=in_specs, out_specs=out_specs, check_vma=False)
```

```python
import functools

import jax
import jax.numpy as jnp
from jax import lax
from jax.experimental import pallas as pl
from jax.experimental.pallas import tpu as pltpu
from jax.sharding import PartitionSpec as P

HEAD_SIZE = 128
PLACES = 4
TICKS = 3
EPS = 1e-05
MESH = pl.DeviceIdType.MESH
LIMIT = 56 * 1024 * 1024
F32 = jnp.float32
B16 = jnp.bfloat16
ACROSS = (((1,), (1,)), ((), ()))
DOWN = (((0,), (0,)), ((), ()))
PLAIN = (((1,), (0,)), ((), ()))


def dot(left, right, dims):
    return lax.dot_general(left, right, dims, preferred_element_type=F32)


def remote(src, dst, send, recv, **where):
    return pltpu.make_async_remote_copy(
        src_ref=src,
        dst_ref=dst,
        send_sem=send,
        recv_sem=recv,
        device_id=where,
        device_id_type=MESH,
    )


def each(low, high, step):
    def one(i, _):
        step(i)
        return 0

    lax.fori_loop(low, high, one, 0)


def relay_kernel(
    n, sections,
    saved_in, cot, w, gains_in, lengths_in, segments_in,
    out, grad, gain_out,
    saved, gains, lengths, segments,
    xs, xin, qb, qh, cotb, metab, gb, w2, parts, far, ends, kvin, own, kvb,
    kcb, statb, qcb, newc, acc, gacc, gsum, gin, held,
    x_s, x_r, c_s, c_r, m_s, m_r, g_s, g_r, w_s, w_r, l_s, re_s, re_r, rk_s, rk_r,
    ag_s, ag_r, st_s, st_r, qh_s, qh_r, kl_s, kl_r, pp_s, pp_r, co_s, co_r, gg_s, gg_r,
    h_s, h_r, in_s,
):
    me = lax.axis_index("fsdp")
    section = lax.axis_index("pipe")
    lanes = n // PLACES
    place, lane = lax.div(me, lanes), lax.rem(me, lanes)
    rows, model = cot.shape
    wide = model // PLACES
    width = w.shape[1]
    half = w.shape[2] // 2
    members = PLACES * rows
    partner = place + 1 - 2 * lax.rem(place, 2)
    upper = lax.div(place, 2)
    is_mid = lax.rem(lax.rem(place, 2) + upper, 2)
    far_mid, far_end = 2 - upper, 3 - 3 * upper
    dests = (lax.rem(place + 2, PLACES), PLACES - 1 - place, partner, place)
    below = lax.rem(section + sections - 1, sections)
    above = lax.rem(section + 1, sections)
    across = lax.rem(section + sections // 2, sections)
    loaded = section < sections // 2

    def layer_of(tick):
        item = lax.rem(section + tick, sections)
        return item, lax.rem(item, 2) * sections + item - tick

    def stretch_of(tick):
        return lax.div(jnp.maximum(layer_of(tick)[1], 0), sections)

    first = stretch_of(0)
    second = 1 - first

    def when_active(tick, step):
        if tick:
            pl.when(layer_of(tick)[1] >= 0)(step)
        else:
            step()

    def at_place(other):
        return other * lanes + lane

    def at_lane(j):
        return place * lanes + lax.rem(lane + j, lanes)

    def cols(start, size):
        return pl.ds(pl.multiple_of(start, size), size)

    loads = [
        pltpu.make_async_copy(saved_in.at[0], saved.at[0], in_s.at[0]),
        pltpu.make_async_copy(lengths_in, lengths, in_s.at[3]),
        pltpu.make_async_copy(segments_in, segments, in_s.at[4]),
        pltpu.make_async_copy(gains_in, gains, in_s.at[5]),
        pltpu.make_async_copy(saved_in.at[1], saved.at[1], in_s.at[1]),
        pltpu.make_async_copy(saved_in.at[2], saved.at[2], in_s.at[2]),
    ]
    for load in loads:
        load.start()

    barrier = pltpu.get_barrier_semaphore()

    def greet(**where):
        pl.semaphore_signal(barrier, inc=1, device_id=where, device_id_type=MESH)

    each(1, PLACES, lambda k: greet(fsdp=at_place(lax.rem(place + k, PLACES))))
    each(1, lanes, lambda j: greet(fsdp=at_lane(j)))
    greet(pipe=below)
    greet(pipe=above)
    greet(pipe=across)
    greet(pipe=across, fsdp=at_place(dests[0]))

    def own_w(i, stretch):
        mine = cols(lane * width, width)
        return pltpu.make_async_copy(w.at[stretch], w2.at[stretch, mine], l_s.at[i])

    own_w(0, first).start()
    own_w(1, second).start()

    def normalize(tick):
        x = saved[tick].astype(F32)
        factor = lax.rsqrt(jnp.mean(x * x, axis=-1, keepdims=True) + EPS)
        xs[tick] = (x * factor).astype(B16)
        item, _ = layer_of(tick)
        turned = jnp.transpose(jnp.broadcast_to(factor, (rows, HEAD_SIZE)))[0:1]
        doc = segments[pl.ds(item, 1), :].astype(F32)
        at = lax.broadcasted_iota(jnp.int32, lengths.shape, 1)
        used = jnp.sum(jnp.where(at == item, lengths[...].astype(F32), 0.0), axis=1, keepdims=True)
        metab[place, tick] = jnp.concatenate(
            [
                jnp.concatenate([turned, turned], axis=1),
                jnp.concatenate([doc, doc], axis=1),
                jnp.broadcast_to(used, (1, HEAD_SIZE)),
                jnp.zeros((5, HEAD_SIZE), F32),
            ],
            axis=0,
        )

    for load in loads[:4]:
        load.wait()
    normalize(0)
    gb[lane] = gains[...].astype(F32)
    pl.semaphore_wait(barrier, PLACES - 1 + lanes - 1 + 4)

    def x_copy(tick, k):
        to = lax.rem(place + k, PLACES)
        return remote(
            xs.at[tick, :, cols(to * wide, wide)], xin.at[tick, place],
            x_s.at[tick, k], x_r.at[tick, k], fsdp=at_place(to),
        )

    def relay_copy(tick):
        return remote(
            xs.at[tick, :, cols(dests[0] * wide, wide)], held.at[tick],
            h_s.at[tick], h_r.at[tick], pipe=across,
        )

    def relayed_copy(tick):
        return remote(
            held.at[tick], xin.at[tick, place],
            h_s.at[tick], x_r.at[tick, 2], pipe=across, fsdp=at_place(dests[0]),
        )

    def start_far(tick):
        @pl.when(section >= sections // 2)
        def _():
            relay_copy(tick).wait_recv()
            relayed_copy(tick).start()
            when_active(tick, lambda: x_copy(tick, 2).start())

    def start_next(tick):
        @functools.partial(when_active, tick)
        def _():
            x_copy(tick, 1).start()
            x_copy(tick, 3).start()

    def cot_copy(k):
        to = lax.rem(place + k, PLACES)
        return remote(
            cot.at[:, cols(to * wide, wide)], cotb.at[0, place],
            c_s.at[k], c_r.at[k], fsdp=at_place(to),
        )

    def meta_copy(tick, k):
        to = lax.rem(place + k, PLACES)
        return remote(
            metab.at[place, tick], metab.at[place, tick],
            m_s.at[tick, k], m_r.at[tick, k], fsdp=at_place(to),
        )

    def gain_copy(j):
        return remote(gb.at[lane], gb.at[lane], g_s.at[j], g_r.at[j], fsdp=at_lane(j))

    def w_copy(i, k, side, j):
        stretch = (first, second)[i]
        here = cols(dests[k] * HEAD_SIZE + side * half, HEAD_SIZE)
        return remote(
            w.at[stretch, :, here], w2.at[stretch, cols(lane * width, width), here],
            w_s.at[i, k, side, j], w_r.at[i, k, side, j], fsdp=at_lane(j),
        )

    def send_w(i):
        for k in range(4):
            for side in range(2):
                each(1, lanes, lambda j: w_copy(i, k, side, j).start())

    each(1, lanes, lambda j: gain_copy(j).start())
    each(1, PLACES, lambda k: x_copy(0, k).start())
    send_w(0)
    each(1, PLACES, lambda k: meta_copy(0, k).start())
    each(1, PLACES, lambda k: cot_copy(k).start())
    send_w(1)

    xin[0, place] = xs[0, :, cols(place * wide, wide)]
    own_cot = pltpu.make_async_copy(cot.at[:, cols(place * wide, wide)], cotb.at[0, place], c_s.at[0])
    own_cot.start()
    for tick in (1, 2):
        loads[3 + tick].wait()
        normalize(tick)
        each(1, PLACES, lambda k: meta_copy(tick, k).start())
        xin[tick, place] = xs[tick, :, cols(place * wide, wide)]

        @pl.when(loaded)
        def _():
            relay_copy(tick).start()

    each(1, lanes, lambda j: gain_copy(j).wait_recv())

    def gain_of(tick):
        stretch = stretch_of(tick)
        return jnp.concatenate(
            [gb[i, pl.ds(stretch, 1), :] for i in range(lanes)], axis=1
        )

    def q_copy(tick, j):
        to = lax.rem(lane + j, lanes)
        return remote(
            qb.at[tick, :, cols(to * width, width)], qh.at[lane, tick],
            qh_s.at[tick, j], qh_r.at[tick, j], fsdp=at_lane(j),
        )

    def end_copy(tick, k):
        return remote(
            parts.at[tick, k], ends.at[tick, k],
            re_s.at[tick, k], re_r.at[tick, k], fsdp=at_place(partner),
        )

    def partner_copy(tick):
        return remote(
            parts.at[tick, 2], kvin.at[tick, 0],
            rk_s.at[tick, 2], rk_r.at[tick, 0], fsdp=at_place(partner),
        )

    def far_copy(tick, k):
        return remote(
            parts.at[tick, k], kvin.at[tick, 1],
            rk_s.at[tick, k], rk_r.at[tick, 1], fsdp=at_place(dests[k]),
        )

    def take_w(i, k):
        for side in range(2):
            each(1, lanes, lambda j: w_copy(i, k, side, j).wait_recv())

    def forward(tick):
        stretch = stretch_of(tick)
        each(1, PLACES, lambda k: x_copy(tick, k).wait_recv())
        q = (xin[tick].reshape(members, wide).astype(F32) * gain_of(tick)).astype(B16)
        qb[tick] = q
        each(1, lanes, lambda j: q_copy(tick, j).start())
        if tick < 2:
            own_w(tick, (first, second)[tick]).wait()
        for k in range(4):
            if tick < 2:
                take_w(tick, k)
            at = [cols(dests[k] * HEAD_SIZE + side * half, HEAD_SIZE) for side in range(2)]
            right = jnp.concatenate([w2[stretch, :, a] for a in at], axis=1)
            part = dot(qb[tick], right, PLAIN)
            if k < 2:
                far[k] = part

                @pl.when(is_mid == 0)
                def _():
                    parts[tick, k] = far[k].astype(B16)
                    end_copy(tick, k).start()

            elif k == 2:
                parts[tick, 2] = part.astype(B16)
                partner_copy(tick).start()
            else:
                own[tick] = part

    def combine(tick):
        @pl.when(is_mid == 1)
        def _():
            for k in range(2):
                end_copy(tick, 1 - k).wait_recv()
                parts[tick, k] = (far[k] + ends[tick, 1 - k].astype(F32)).astype(B16)
                far_copy(tick, k).start()

    def gather_kv(tick):
        partner_copy(tick).wait_recv()
        far_copy(tick, 0).wait_recv()
        total = own[tick] + kvin[tick, 0].astype(F32) + kvin[tick, 1].astype(F32)
        kvb[tick] = total.astype(B16).reshape(PLACES, rows, 2 * HEAD_SIZE)

    def pipe_copy(tick, m):
        return remote(
            newc.at[tick, m], cotb.at[tick + 1, m],
            pp_s.at[tick, m], pp_r.at[tick, m], pipe=below,
        )

    def near_copies(tick, m, which=(0, 1)):
        chunk, stat = kcb.at[lane, tick, place, m], statb.at[tick, place, m]
        copies = []
        for i in which:
            to, slot = ((partner, 0), (far_mid, 2 - is_mid))[i]
            for ref, send, recv in ((chunk, ag_s, ag_r), (stat, st_s, st_r)):
                copies.append(
                    remote(ref, ref, send.at[tick, m, i], recv.at[tick, m, slot],
                           fsdp=at_place(to))
                )
        return copies

    def pass_copies(tick, m, slot):
        source = (far_mid, far_end)[slot - 1]
        chunk, stat = kcb.at[lane, tick, source, m], statb.at[tick, source, m]
        return [
            remote(chunk, chunk, ag_s.at[tick, m, 1 + slot], ag_r.at[tick, m, slot],
                   fsdp=at_place(partner)),
            remote(stat, stat, st_s.at[tick, m, 1 + slot], st_r.at[tick, m, slot],
                   fsdp=at_place(partner)),
        ]

    def pass_on(tick, m):
        @pl.when(is_mid == 1)
        def _():
            for slot in (1, 2):
                for copy in pass_copies(tick, m, slot):
                    copy.wait_recv()
                    copy.start()

    def heads(value):
        return jnp.concatenate(
            [
                value[:, i * HEAD_SIZE : (i + 1) * HEAD_SIZE]
                for i in range(wide // HEAD_SIZE)
            ],
            axis=0,
        )

    groups = wide // HEAD_SIZE
    scale = HEAD_SIZE ** (-0.5)

    def attend(tick, m):
        if tick:
            pipe_copy(tick - 1, m).wait_recv()
        query = heads(qb[tick, pl.ds(pl.multiple_of(m * rows, rows), rows), :])
        pulled = heads(cotb[tick, m])
        keys = kvb[tick, m, :, :HEAD_SIZE]
        values = kvb[tick, m, :, HEAD_SIZE:]
        meta = metab[m, tick]
        turned = jnp.transpose(meta)

        def tiled(row):
            return jnp.concatenate([meta[row : row + 1]] * (groups * rows // HEAD_SIZE), axis=1)

        shape = (rows, groups * rows)
        spot = lax.broadcasted_iota(jnp.int32, shape, 0)
        seer = lax.rem(lax.broadcasted_iota(jnp.int32, shape, 1), rows)
        key_spot = lax.broadcasted_iota(jnp.int32, (rows, 1), 0).astype(F32)
        doc = jnp.where(key_spot < turned[:rows, 2:3], turned[:rows, 1:2], -1.0)
        seen = ((doc == tiled(1)) & (spot <= seer)) | (spot == seer)
        row_spot = seer[0:1].astype(F32)
        valid = jnp.where(row_spot < tiled(2), 1.0, 0.0)
        raw = dot(keys, query, ACROSS)
        scores = jnp.where(seen, raw * scale, -1e30)
        expo = jnp.exp(scores - jnp.max(scores, axis=0, keepdims=True))
        probs = expo / jnp.sum(expo, axis=0, keepdims=True)
        prob_cot = dot(values, pulled, ACROSS).astype(B16).astype(F32) * valid
        inner = jnp.sum(probs * prob_cot, axis=0, keepdims=True)
        score_cot = jnp.where(seen, probs * (prob_cot - inner), 0.0) * scale
        score_b = score_cot.astype(B16)
        query_cot = dot(score_b, keys, DOWN)
        for i in range(groups):
            qcb[m, :, i * HEAD_SIZE : (i + 1) * HEAD_SIZE] = query_cot[
                i * rows : (i + 1) * rows
            ].astype(B16)
        key_cot = dot(score_b, query, PLAIN).astype(B16)
        value_cot = dot((probs * valid).astype(B16), pulled, PLAIN).astype(B16)
        kcb[lane, tick, place, m, :, :HEAD_SIZE] = key_cot
        kcb[lane, tick, place, m, :, HEAD_SIZE:] = value_cot
        line = jnp.sum(score_cot * raw, axis=0, keepdims=True)
        while line.shape[1] > HEAD_SIZE:
            cut = line.shape[1] // 2
            line = line[:, :cut] + line[:, cut:]
        line = line + pltpu.roll(line, rows, 1)
        both = keys.astype(F32) * key_cot.astype(F32) + values.astype(F32) * value_cot.astype(F32)
        high = both.astype(B16)
        low = (both - high.astype(F32)).astype(B16)
        ones = jnp.ones((8, HEAD_SIZE), B16)
        flat = dot(ones, high, ACROSS) + dot(ones, low, ACROSS)
        statb[tick, place, m] = jnp.concatenate([flat, flat], axis=1) + line
        for copy in near_copies(tick, m):
            copy.start()

    def lane_copy(tick, m, j):
        chunk = kcb.at[lane, tick, :, m]
        return remote(chunk, chunk, kl_s.at[tick, m, j], kl_r.at[tick, m, j], fsdp=at_lane(j))

    def out_copy(m):
        return remote(
            newc.at[TICKS - 1, m], out.at[:, cols(place * wide, wide)],
            co_s.at[m], co_r.at[place], fsdp=at_place(m),
        )

    def settle(tick, m):
        stretch = stretch_of(tick)
        for copy in near_copies(tick, m, (0,)):
            copy.wait_recv()

        @pl.when(is_mid == 0)
        def _():
            for slot in (1, 2):
                for copy in pass_copies(tick, m, slot):
                    copy.wait_recv()

        each(1, lanes, lambda j: lane_copy(tick, m, j).start())
        kc = jnp.concatenate(
            [
                kcb[lane, tick, d, m, :, side * HEAD_SIZE : (side + 1) * HEAD_SIZE]
                for side in range(2)
                for d in range(PLACES)
            ],
            axis=1,
        )
        total = qcb[m].astype(F32) + dot(kc, w2[stretch], ACROSS)
        stat = statb[tick, 0, m]
        for d in range(1, PLACES):
            stat = stat + statb[tick, d, m]
        mean = jnp.transpose(stat)[:rows, 0:1] * (1.0 / model)
        factor = jnp.transpose(metab[m, tick])[:rows, 0:1]
        xhat = xin[tick, m].astype(F32)
        gain = gain_of(tick)
        gacc[stretch] += jnp.sum((xhat * total).reshape(rows // 8, 8, wide), axis=0)
        x_cot = factor * (gain * total - xhat * mean)
        fresh = (cotb[tick, m].astype(F32) + x_cot).astype(B16)
        newc[tick, m] = fresh
        hand_down(tick, m)

    def relay_out(m):
        return remote(
            newc.at[TICKS - 1, m], held.at[0], h_s.at[0], h_r.at[0], pipe=across
        )

    def relayed_out():
        return remote(
            held.at[0], out.at[:, cols(place * wide, wide)],
            h_s.at[0], co_r.at[place], pipe=across, fsdp=at_place(dests[0]),
        )

    def hand_down(tick, m):
        if tick < TICKS - 1:
            pipe_copy(tick, m).start()
        else:

            @pl.when(m == place)
            def _():
                out[:, cols(place * wide, wide)] = newc[tick, m]

            relayed = loaded & (m == dests[0])

            @pl.when(relayed)
            def _():
                relay_out(m).start()

            @pl.when((m != place) & jnp.logical_not(relayed))
            def _():
                out_copy(m).start()

    def weigh(tick):
        stretch = stretch_of(tick)
        qh[lane, tick] = qb[tick, :, cols(lane * width, width)]
        each(1, lanes, lambda j: q_copy(tick, j).wait_recv())
        each(0, PLACES, lambda m: each(1, lanes, lambda j: lane_copy(tick, m, j).wait_recv()))

        def one(d):
            total = acc[stretch, d]
            for i in range(lanes):
                right = kcb[i, tick, d].reshape(members, 2 * HEAD_SIZE)
                total = total + dot(qh[i, tick], right, DOWN)
            acc[stretch, d] = total

        each(0, PLACES, one)

    forward(0)
    start_next(1)
    combine(0)
    start_far(1)
    acc[...] = jnp.zeros_like(acc)
    gacc[...] = jnp.zeros_like(gacc)
    each(1, PLACES, lambda k: meta_copy(0, k).wait_recv())
    each(1, PLACES, lambda k: cot_copy(k).wait_recv())
    own_cot.wait()
    for tick in range(TICKS):

        @functools.partial(when_active, tick)
        def _():
            gather_kv(tick)
            each(0, PLACES, lambda m: attend(tick, m))
            pass_on(tick, 0)

        if tick == TICKS - 1:
            weigh(0)
        if tick < TICKS - 1:
            when_active(tick + 1, lambda: forward(tick + 1))
        if tick == 0:

            @pl.when(layer_of(1)[1] < 0)
            def _():
                own_w(1, second).wait()
                for k in range(4):
                    take_w(1, k)

        if tick == 0:
            start_far(2)

        def step(i):
            @pl.when(i < PLACES - 1)
            def _():
                pass_on(tick, i + 1)

            settle(tick, i)

        when_active(tick, lambda: each(0, PLACES, step))
        if tick:

            def unchanged(m):
                pipe_copy(tick - 1, m).wait_recv()
                newc[tick, m] = cotb[tick, m]
                hand_down(tick, m)

            pl.when(layer_of(tick)[1] < 0)(lambda: each(0, PLACES, unchanged))
        if tick == 0:
            start_next(2)
        if tick < TICKS - 1:
            when_active(tick + 1, lambda: combine(tick + 1))
            each(1, PLACES, lambda k: meta_copy(tick + 1, k).wait_recv())

    gain_sum = jnp.sum(gacc[...], axis=1)
    for i in range(lanes):
        gsum[i] = gain_sum[:, i * width : (i + 1) * width]

    def sum_copy(j):
        to = lax.rem(lane + j, lanes)
        return remote(gsum.at[to], gin.at[lane], gg_s.at[j], gg_r.at[j], fsdp=at_lane(j))

    each(1, lanes, lambda j: sum_copy(j).start())
    gin[lane] = gsum[lane]
    when_active(TICKS - 2, lambda: weigh(TICKS - 2))
    when_active(TICKS - 1, lambda: weigh(TICKS - 1))

    @pl.when(jnp.logical_not(loaded))
    def _():
        relay_out(dests[0]).wait_recv()
        relayed_out().start()

    for d in range(PLACES):
        for side in range(2):
            start = d * HEAD_SIZE + side * half
            grad[:, :, start : start + HEAD_SIZE] = acc[
                :, d, :, side * HEAD_SIZE : (side + 1) * HEAD_SIZE
            ].astype(B16)
    each(1, lanes, lambda j: sum_copy(j).wait())
    gain_out[...] = jnp.sum(gin[...], axis=0).astype(B16)

    def out_wait(k):
        to = lax.rem(place + k, PLACES)
        if k == 2:
            relay_out(to).wait_send()
            pl.when(jnp.logical_not(loaded))(lambda: out_copy(to).wait_send())
        else:
            out_copy(to).wait_send()
        remote(
            newc.at[TICKS - 1, to], out.at[:, cols(to * wide, wide)],
            co_s.at[to], co_r.at[to], fsdp=at_place(to),
        ).wait_recv()

    for k in range(1, PLACES):
        out_wait(k)
    each(1, PLACES, lambda k: cot_copy(k).wait_send())
    each(1, lanes, lambda j: gain_copy(j).wait_send())
    for side in range(2):
        for i in range(2):
            for k in range(4):
                each(1, lanes, lambda j: w_copy(i, k, side, j).wait_send())
    for tick in range(TICKS):
        each(1, PLACES, lambda k: meta_copy(tick, k).wait_send())
        if tick:
            relay_copy(tick).wait_send()
        if tick < TICKS - 1:
            each(0, PLACES, lambda m: pipe_copy(tick, m).wait_send())

        @functools.partial(when_active, tick)
        def _():
            if tick:
                x_copy(tick, 1).wait_send()
                pl.when(jnp.logical_not(loaded))(lambda: x_copy(tick, 2).wait_send())
                x_copy(tick, 3).wait_send()
            else:
                each(1, PLACES, lambda k: x_copy(tick, k).wait_send())
            each(1, lanes, lambda j: q_copy(tick, j).wait_send())
            partner_copy(tick).wait_send()

            def finish(m):
                for copy in near_copies(tick, m):
                    copy.wait_send()
                each(1, lanes, lambda j: lane_copy(tick, m, j).wait_send())

                @pl.when(is_mid == 1)
                def _():
                    for slot in (1, 2):
                        for copy in pass_copies(tick, m, slot):
                            copy.wait_send()

            each(0, PLACES, finish)

            @pl.when(is_mid == 1)
            def _():
                for k in range(2):
                    far_copy(tick, k).wait_send()

            @pl.when(is_mid == 0)
            def _():
                for k in range(2):
                    end_copy(tick, k).wait_send()


def relay(n, sections, saved, cot, w, gains, lengths, segments):
    ticks, rows, model = saved.shape
    width, kvw = w.shape[1:]
    lanes = n // PLACES
    wide = model // PLACES
    members = PLACES * rows
    pair = 2 * HEAD_SIZE
    vmem = pl.BlockSpec(memory_space=pltpu.VMEM)
    dma = pltpu.SemaphoreType.DMA
    return pl.pallas_call(
        functools.partial(relay_kernel, n, sections),
        out_shape=(
            jax.ShapeDtypeStruct((rows, model), B16),
            jax.ShapeDtypeStruct(w.shape, B16),
            jax.ShapeDtypeStruct(gains.shape, B16),
        ),
        in_specs=[pl.BlockSpec(memory_space=pltpu.HBM)] * 6,
        out_specs=(vmem,) * 3,
        scratch_shapes=[
            pltpu.VMEM(saved.shape, B16),
            pltpu.VMEM(gains.shape, B16),
            pltpu.VMEM(lengths.shape, jnp.int32),
            pltpu.VMEM(segments.shape, jnp.int32),
            pltpu.VMEM((ticks, rows, model), B16),
            pltpu.VMEM((ticks, PLACES, rows, wide), B16),
            pltpu.VMEM((ticks, members, wide), B16),
            pltpu.VMEM((lanes, ticks, members, width), B16),
            pltpu.VMEM((ticks, PLACES, rows, wide), B16),
            pltpu.VMEM((PLACES, ticks, 8, HEAD_SIZE), F32),
            pltpu.VMEM((lanes, 2, width), F32),
            pltpu.VMEM((2, lanes * width, kvw), B16),
            pltpu.VMEM((ticks, 3, members, pair), B16),
            pltpu.VMEM((2, members, pair), F32),
            pltpu.VMEM((ticks, 2, members, pair), B16),
            pltpu.VMEM((ticks, 2, members, pair), B16),
            pltpu.VMEM((ticks, members, pair), F32),
            pltpu.VMEM((ticks, PLACES, rows, pair), B16),
            pltpu.VMEM((lanes, ticks, PLACES, PLACES, rows, pair), B16),
            pltpu.VMEM((ticks, PLACES, PLACES, 8, HEAD_SIZE), F32),
            pltpu.VMEM((PLACES, rows, wide), B16),
            pltpu.VMEM((ticks, PLACES, rows, wide), B16),
            pltpu.VMEM((2, PLACES, width, pair), F32),
            pltpu.VMEM((2, 8, wide), F32),
            pltpu.VMEM((lanes, 2, width), F32),
            pltpu.VMEM((lanes, 2, width), F32),
            pltpu.VMEM((ticks, rows, wide), B16),
        ]
        + [dma((ticks, PLACES))] * 2
        + [dma((PLACES,))] * 2
        + [dma((ticks, PLACES))] * 2
        + [dma((lanes,))] * 2
        + [dma((2, 4, 2, lanes))] * 2
        + [dma((2,))]
        + [dma((ticks, 2))] * 2
        + [dma((ticks, 3)), dma((ticks, 2))]
        + [dma((ticks, PLACES, 4)), dma((ticks, PLACES, 3))]
        + [dma((ticks, PLACES, 4)), dma((ticks, PLACES, 3))]
        + [dma((ticks, lanes))] * 2
        + [dma((ticks, PLACES, lanes))] * 2
        + [dma((ticks, PLACES))] * 2
        + [dma((PLACES,))] * 2
        + [dma((lanes,))] * 2
        + [dma((ticks,))] * 2
        + [dma((6,))],
        compiler_params=pltpu.CompilerParams(
            collective_id=0, has_side_effects=True, vmem_limit_bytes=LIMIT
        ),
    )(saved, cot, w, gains, lengths, segments)


def handed_on_kernel(out, grad, gain, to_out, to_grad, to_gain, out_v, grad_v, gain_v, sems):
    half = grad.shape[1] // 2
    routes = [(out, out_v, to_out), (gain, gain_v, to_gain)]
    for stretch in range(2):
        for start in (0, half):
            routes.append([ref.at[stretch, start : start + half] for ref in (grad, grad_v, to_grad)])
    ins = [pltpu.make_async_copy(a, b, sems.at[0, i]) for i, (a, b, _) in enumerate(routes)]
    outs = [pltpu.make_async_copy(b, c, sems.at[1, i]) for i, (_, b, c) in enumerate(routes)]
    for copy in ins:
        copy.start()
    for i, copy in enumerate(outs):
        ins[i].wait()
        copy.start()
    for copy in outs:
        copy.wait()


def handed_on(*values):
    anywhere = pl.BlockSpec(memory_space=pl.ANY)
    return pl.pallas_call(
        handed_on_kernel,
        out_shape=tuple(jax.ShapeDtypeStruct(v.shape, v.dtype) for v in values),
        in_specs=[anywhere] * len(values),
        out_specs=(anywhere,) * len(values),
        scratch_shapes=[pltpu.VMEM(v.shape, v.dtype) for v in values]
        + [pltpu.SemaphoreType.DMA((2, 6))],
        compiler_params=pltpu.CompilerParams(vmem_limit_bytes=LIMIT),
    )(*values)


def body(saved, cot_in, weights, gains, lengths, segments):
    out, grad_kv, grad_gain = relay(
        lax.axis_size("fsdp"), lax.axis_size("pipe"),
        saved[0, 0], cot_in[0, 0], weights[:, 0], gains[:, 0], lengths.T, segments[:, 0],
    )
    out, grad_kv, grad_gain = handed_on(out, grad_kv, grad_gain)
    return out[None, None], grad_kv[:, None], grad_gain[:, None]


def solution(mesh):
    in_specs = (
        P("pipe", "fsdp", None, None, None),
        P("pipe", "fsdp", None, None),
        P(None, "pipe", "fsdp", None),
        P(None, "pipe", "fsdp"),
        P(None, "fsdp"),
        P(None, "fsdp", None),
    )
    out_specs = (
        P("pipe", "fsdp", None, None),
        P(None, "pipe", "fsdp", None),
        P(None, "pipe", "fsdp"),
    )
    return jax.shard_map(body, mesh=mesh, in_specs=in_specs, out_specs=out_specs, check_vma=False)
```
